512 devices in a mesh: gx: 32 (over z_lo, y), gy: 16 (over x, z_hi, core).
Axes of the slice: x: 4, y: 8, z: 8 (z_hi: 2, z_lo: 4; z = z_hi * 4 + z_lo), core: 2. Of those that a mesh axis runs over, the one named last changes fastest.
Arguments:
- forward_pops: float32 [19, 256, 256, 128], P(None, 'gx', 'gy'), may hold values from 0.005 to 1, as said below
- later_adjoint: float32 [19, 256, 256, 128], P(None, 'gx', 'gy'), may hold values from -6 to 6
- design: float32 [256, 256, 128], P('gx', 'gy'), may hold values from 0 to 1
- node_type: int32 [256, 256, 128], P('gx', 'gy'), may hold values from 0 to 4, as said below
- region: int32 [256, 256, 128], P('gx', 'gy'), may hold values from 0 to 7
Outputs:
- adjoint: float32 [19, 256, 256, 128], P(None, 'gx', 'gy')
- sensitivity: float32 [256, 256, 128], P('gx', 'gy')
- objective: float32 [], replicated
- volumes: float32 [8], replicated
The draws below stay inside these ranges and needn't reach their ends.
Inputs may be any that keep to these rules, and one draw needn't show every extreme that they name: `node_type`: 0 fluid, 1 design, 2 wall, 3 inlet, 4 outlet. `forward_pops`: positive populations.
All inputs are finite; a program needn't handle non-finite values.
Results may differ from the reference program's by a relative error of at most 0.00002.
Values sent between devices are 32-bit elements; how exact they have to be, the bound alone decides.
No kernel may reach another device: no remote copies, remote signals or barrier semaphores. Data moves between devices by JAX's collectives and lax.ppermute only.
A program may use at most 64 MiB of HBM per device.

```python
import math
import jax
import jax.numpy as jnp

Q = 19
NZ = 128
RAD = 3
REG = 8
NX = 256
NY = 256


WEIGHT_LIST = [1.0 / 3.0] + [1.0 / 18.0] * 6 + [1.0 / 36.0] * 12


XDIR_LIST = [0.0, 1.0, -1.0, 0.0, 0.0, 0.0, 0.0, 1.0, -1.0, 1.0, -1.0, 1.0, -1.0, 1.0, -1.0, 0.0, 0.0, 0.0, 0.0]


def draw_forward_pops(key, part):
    table = jnp.array(WEIGHT_LIST, jnp.float32)[:, None, None, None]
    xdir = jnp.array(XDIR_LIST, jnp.float32)[:, None, None, None]
    spread_noise = jnp.exp(jax.random.uniform(key, (Q, NX, NY, NZ), jnp.float32, -0.5, 0.5))
    return table * (1.0 + 0.3 * xdir) * spread_noise


def draw_design(key, part):
    key_power = jax.random.fold_in(key, 11)
    key_base = jax.random.fold_in(key, 12)
    exponent = jnp.exp(jax.random.uniform(key_power, (NX, NY, 1), jnp.float32, math.log(0.3), math.log(3.0)))
    uniform_base = jax.random.uniform(key_base, (NX, NY, NZ), jnp.float32, 0.0, 1.0)
    return jnp.power(uniform_base, exponent)


def draw_node_type(key, part):
    draw_code = jax.random.randint(key, (NX, NY, NZ), 0, 16)
    return jnp.where(draw_code < 7, 0, jnp.where(draw_code < 13, 1, draw_code - 11)).astype(jnp.int32)


def place_ends(values, rng, low, largest):
    place = [jax.random.randint(jax.random.fold_in(rng, axis), (), 0, length) for axis, length in enumerate(values.shape)]
    main_axis = values.shape.index(max(values.shape))
    neighbour = place[:main_axis] + [(place[main_axis] + 1) % values.shape[main_axis]] + place[main_axis + 1:]
    return values.at[tuple(place)].set(low).at[tuple(neighbour)].set(largest)


def steps_of(key, shape, shards, least, top_value):
    def one(position, shards_of):
        steps = jax.random.uniform(jax.random.fold_in(jax.random.fold_in(key, 6), position), (shards_of,), jnp.float32, least / len(shards), top_value / len(shards))
        return jnp.repeat(jnp.exp(steps), shape[position] // shards_of).reshape((-1,) + (1,) * (len(shape) - position - 1))

    factor_of = one(*shards[0])
    for cut in shards[1:]:
        factor_of = factor_of * one(*cut)
    return factor_of


def noise(key, dims, deviation, reach, cuts=(), kind=jnp.bfloat16):
    level = steps_of(key, dims, cuts, -0.22, 0.18) if cuts else 1.0
    values = jax.random.normal(key, dims, jnp.float32) * deviation * level
    return jnp.minimum(jnp.maximum(values, -reach), reach).astype(kind)


def setup_inputs(seed: int = 0) -> dict:
    key_list = jax.random.split(jax.random.key(seed), 6)
    return {
        "forward_pops": draw_forward_pops(jax.random.fold_in(key_list[5], 71), 0),
        "later_adjoint": noise(key_list[1], (Q, NX, NY, NZ), 1.0, 6.0, ((1, 32), (2, 16)), jnp.float32),
        "design": draw_design(jax.random.fold_in(key_list[5], 71), 0),
        "node_type": draw_node_type(jax.random.fold_in(key_list[5], 71), 0),
        "region": place_ends(jax.random.randint(key_list[4], (NX, NY, NZ), 0, REG), jax.random.fold_in(key_list[4], 1), 0, REG - 1).astype(jnp.int32),
    }


VELOCITY = [(0, 0, 0), (1, 0, 0), (-1, 0, 0), (0, 1, 0), (0, -1, 0), (0, 0, 1), (0, 0, -1), (1, 1, 0), (-1, -1, 0), (1, -1, 0), (-1, 1, 0), (1, 0, 1), (-1, 0, -1), (1, 0, -1), (-1, 0, 1), (0, 1, 1), (0, -1, -1), (0, 1, -1), (0, -1, 1)]
WEIGHTS = [1.0 / 3.0] + [1.0 / 18.0] * 6 + [1.0 / 36.0] * 12
OPPOSITE = [0, 2, 1, 4, 3, 6, 5, 8, 7, 10, 9, 12, 11, 14, 13, 16, 15, 18, 17]
RELAXATION = 1.0 / 0.6
BRINKMAN = 0.9

def moments(populations):
    density = populations[0]
    for i in range(1, 19):
        density = density + populations[i]
    momenta = []
    for a in range(3):
        running = jnp.zeros_like(density)
        for i in range(19):
            if VELOCITY[i][a] == 1:
                running = running + populations[i]
            elif VELOCITY[i][a] == -1:
                running = running - populations[i]
        momenta.append(running)
    return (density, momenta)

def projections(velocity):
    result = []
    for i in range(19):
        running = jnp.zeros_like(velocity[0])
        for a in range(3):
            if VELOCITY[i][a] != 0:
                running = running + VELOCITY[i][a] * velocity[a]
        result.append(running)
    return result

def rates(kind):
    return jnp.where(kind <= 1, RELAXATION, 1.0)

def collide(populations, kind, factor):
    density, momenta = moments(populations)
    plain = [m / density for m in momenta]
    velocity = [factor * p for p in plain]
    speed_sq = velocity[0] * velocity[0] + velocity[1] * velocity[1] + velocity[2] * velocity[2]
    along = projections(velocity)
    omega_cell = rates(kind)
    wall = kind == 2
    output = []
    for i in range(19):
        balance = WEIGHTS[i] * density * (1.0 + 3.0 * along[i] + 4.5 * along[i] * along[i] - 1.5 * speed_sq)
        relaxed = (1.0 - omega_cell) * populations[i] + omega_cell * balance
        output.append(jnp.where(wall, populations[OPPOSITE[i]], relaxed))
    return jnp.stack(output)

def adjoint_collide(incoming, populations, kind, factor):
    density, momenta = moments(populations)
    plain = [m / density for m in momenta]
    velocity = [factor * p for p in plain]
    speed_sq = velocity[0] * velocity[0] + velocity[1] * velocity[1] + velocity[2] * velocity[2]
    along = projections(velocity)
    omega_cell = rates(kind)
    wall = kind == 2
    scalar_part = jnp.zeros_like(density)
    vector_part = [jnp.zeros_like(density), jnp.zeros_like(density), jnp.zeros_like(density)]
    for j in range(19):
        weighted = WEIGHTS[j] * incoming[j]
        scalar_part = scalar_part + weighted * (1.0 + 3.0 * along[j] + 4.5 * along[j] * along[j] - 1.5 * speed_sq)
        for a in range(3):
            vector_part[a] = vector_part[a] + weighted * (3.0 * VELOCITY[j][a] + 9.0 * along[j] * VELOCITY[j][a] - 3.0 * velocity[a])
    output = []
    for i in range(19):
        coupling = scalar_part
        for a in range(3):
            coupling = coupling + vector_part[a] * (factor * VELOCITY[i][a] - velocity[a])
        relaxed = (1.0 - omega_cell) * incoming[i] + omega_cell * coupling
        output.append(jnp.where(wall, incoming[OPPOSITE[i]], relaxed))
    inner = vector_part[0] * plain[0] + vector_part[1] * plain[1] + vector_part[2] * plain[2]
    gradient = jnp.where(wall, 0.0, omega_cell * density * inner)
    return (jnp.stack(output), gradient)

def displace(extended, sign):
    padded = jnp.pad(extended, ((0, 0), (0, 0), (0, 0), (1, 1)))
    span_x = extended.shape[1] - 2
    span_y = extended.shape[2] - 2
    span_z = extended.shape[3]
    pieces = []
    for i in range(19):
        off_x = 1 + sign * VELOCITY[i][0]
        off_y = 1 + sign * VELOCITY[i][1]
        off_z = 1 + sign * VELOCITY[i][2]
        pieces.append(padded[i, off_x:off_x + span_x, off_y:off_y + span_y, off_z:off_z + span_z])
    return jnp.stack(pieces)

def wrap_rim(populations):
    return jnp.pad(populations, ((0, 0), (1, 1), (1, 1), (0, 0)), mode='wrap')

def filter_taps(padded):
    span_x = padded.shape[0] - 2 * RAD
    span_y = padded.shape[1] - 2 * RAD
    span_z = padded.shape[2] - 2 * RAD
    running = jnp.zeros((span_x, span_y, span_z), jnp.float32)
    for a in range(-RAD, RAD + 1):
        for b in range(-RAD, RAD + 1):
            for c in range(-RAD, RAD + 1):
                weight = RAD + 1 - math.sqrt(a * a + b * b + c * c)
                if weight > 0:
                    running = running + weight * padded[RAD + a:RAD + a + span_x, RAD + b:RAD + b + span_y, RAD + c:RAD + c + span_z]
    return running

def filter_norm(depth):
    block = jnp.pad(jnp.ones((2 * RAD + 1, 2 * RAD + 1, depth), jnp.float32), ((0, 0), (0, 0), (RAD, RAD)))
    return filter_taps(block)

def density_filter(field):
    padded = jnp.pad(field, ((RAD, RAD), (RAD, RAD), (0, 0)), mode='wrap')
    return filter_taps(jnp.pad(padded, ((0, 0), (0, 0), (RAD, RAD))))

def reference(forward_pops, later_adjoint, design, node_type, region):
    norm_field = filter_norm(design.shape[2])
    filtered = density_filter(design) / norm_field
    factor = jnp.where(node_type == 1, 1.0 - BRINKMAN * (1.0 - filtered), 1.0)
    post = collide(forward_pops, node_type, factor)
    next_pops = displace(wrap_rim(post), -1)
    density, momenta = moments(next_pops)
    objective = jnp.sum(jnp.where(node_type == 4, momenta[0], 0.0))
    volumes = jnp.stack([jnp.sum(jnp.where((node_type == 1) & (region == r), filtered, 0.0)) for r in range(REG)])
    incoming = displace(wrap_rim(later_adjoint), 1)
    middle, first_grad = adjoint_collide(incoming, next_pops, node_type, factor)
    source = jnp.where(node_type == 4, 1.0, 0.0)
    middle = middle + jnp.stack([VELOCITY[i][0] * source for i in range(19)])
    incoming = displace(wrap_rim(middle), 1)
    adjoint, second_grad = adjoint_collide(incoming, forward_pops, node_type, factor)
    raw = jnp.where(node_type == 1, BRINKMAN * (first_grad + second_grad), 0.0) / norm_field
    sensitivity = density_filter(raw)
    return (adjoint, sensitivity, objective, volumes)
```

```python
import math

import jax
import jax.numpy as jnp
from jax import lax
from jax.experimental import pallas as pl
from jax.experimental.pallas import tpu as pltpu
from jax.sharding import PartitionSpec as P

RAD = 3
REG = 8
VELOCITY = [
    (0, 0, 0),
    (1, 0, 0),
    (-1, 0, 0),
    (0, 1, 0),
    (0, -1, 0),
    (0, 0, 1),
    (0, 0, -1),
    (1, 1, 0),
    (-1, -1, 0),
    (1, -1, 0),
    (-1, 1, 0),
    (1, 0, 1),
    (-1, 0, -1),
    (1, 0, -1),
    (-1, 0, 1),
    (0, 1, 1),
    (0, -1, -1),
    (0, 1, -1),
    (0, -1, 1),
]
WEIGHTS = [1.0 / 3.0] + [1.0 / 18.0] * 6 + [1.0 / 36.0] * 12
OPPOSITE = [0, 2, 1, 4, 3, 6, 5, 8, 7, 10, 9, 12, 11, 14, 13, 16, 15, 18, 17]
RELAXATION = 1.0 / 0.6
BRINKMAN = 0.9
Q = 19
BX = 8
BY = 16
NZ = 128
F32 = jnp.float32

XP = tuple(i for i in range(Q) if VELOCITY[i][0] == 1)
XM = tuple(i for i in range(Q) if VELOCITY[i][0] == -1)
YP = tuple(i for i in range(Q) if VELOCITY[i][1] == 1)
YM = tuple(i for i in range(Q) if VELOCITY[i][1] == -1)

NODE, DENS, FWD, ADJ, MSG = 4, 5, 9, 14, 19

CLASSES = sorted(
    {a * a + b * b for a in range(RAD + 1) for b in range(RAD + 1) if a * a + b * b < (RAD + 1) ** 2}
)
TAPS = {
    s: [
        (a, b)
        for a in range(-RAD, RAD + 1)
        for b in range(-RAD, RAD + 1)
        if a * a + b * b == s
    ]
    for s in CLASSES
}


def tap_weight(s, c):
    return RAD + 1 - math.sqrt(s + c * c)


def lanes(shape):
    return lax.broadcasted_iota(jnp.int32, shape, len(shape) - 1)


def shift_z(value, c):
    if c == 0:
        return value
    z = lanes(value.shape)
    moved = pltpu.roll(value, (-c) % NZ, value.ndim - 1)
    return jnp.where((z + c >= 0) & (z + c < NZ), moved, 0.0)


def norm_row(shape):
    z = lanes(shape)
    result = None
    for c in range(RAD + 1):
        total = sum(len(TAPS[s]) * tap_weight(s, c) for s in CLASSES if tap_weight(s, c) > 0)
        if c == 0:
            result = jnp.full(shape, total, F32)
        else:
            result = result + jnp.where(z >= c, total, 0.0) + jnp.where(z < NZ - c, total, 0.0)
    return result


def filter_rows(load):
    sums = []
    for s in CLASSES:
        running = None
        for a, b in TAPS[s]:
            tile = load(a, b)
            running = tile if running is None else running + tile
        sums.append(running)
    result = None
    for c in range(RAD + 1):
        mixed = None
        for s, part in zip(CLASSES, sums):
            if tap_weight(s, c) > 0:
                term = tap_weight(s, c) * part
                mixed = term if mixed is None else mixed + term
        if c == 0:
            result = mixed
        else:
            result = result + shift_z(mixed, c) + shift_z(mixed, -c)
    return result


def add_all(values):
    values = list(values)
    while len(values) > 1:
        values = [
            values[k] + values[k + 1] if k + 1 < len(values) else values[k]
            for k in range(0, len(values), 2)
        ]
    return values[0]


def moments(p):
    momenta = []
    for a in range(3):
        up = add_all(p[i] for i in range(Q) if VELOCITY[i][a] == 1)
        down = add_all(p[i] for i in range(Q) if VELOCITY[i][a] == -1)
        momenta.append(up - down)
    return add_all(p), momenta


def along(i, vector):
    result = None
    for a in range(3):
        c = VELOCITY[i][a]
        if c == 0:
            continue
        if result is None:
            result = vector[a] if c == 1 else -vector[a]
        else:
            result = result + vector[a] if c == 1 else result - vector[a]
    return result


def post_tiles(which, straight, bounced, density, momenta, node, factor):
    inverse = 1.0 / density
    u = [factor * (m * inverse) for m in momenta]
    rest = 1.0 - 1.5 * (u[0] * u[0] + u[1] * u[1] + u[2] * u[2])
    rate = jnp.where(node <= 1.5, RELAXATION, 1.0)
    keep = 1.0 - rate
    wall = node == 2.0
    scale = rate * density
    result = {}
    for i in which:
        a = along(i, u)
        form = rest if a is None else rest + a * (3.0 + 4.5 * a)
        relaxed = keep * straight[i] + (WEIGHTS[i] * scale) * form
        result[i] = jnp.where(wall, bounced[i], relaxed)
    return result


def back_tiles(m, density, plain, node, factor):
    u = [factor * q for q in plain]
    rate = jnp.where(node <= 1.5, RELAXATION, 1.0)
    keep = 1.0 - rate
    wall = node == 2.0

    def weighted(select):
        total = None
        for w, group in ((1.0 / 18.0, range(1, 7)), (1.0 / 36.0, range(7, Q))):
            up = [m[i] for i in group if select(VELOCITY[i]) > 0]
            down = [m[i] for i in group if select(VELOCITY[i]) < 0]
            if not up and not down:
                continue
            value = add_all(up)
            if down:
                value = value - add_all(down)
            value = w * value
            total = value if total is None else total + value
        return total

    zero = (1.0 / 3.0) * m[0] + weighted(lambda c: 1)
    one = [weighted(lambda c, a=a: c[a]) for a in range(3)]
    two = {}
    for a in range(3):
        for b in range(a, 3):
            two[a, b] = two[b, a] = weighted(lambda c, a=a, b=b: c[a] * c[b])
    bent = [two[a, 0] * u[0] + two[a, 1] * u[1] + two[a, 2] * u[2] for a in range(3)]
    dot = lambda p, q: p[0] * q[0] + p[1] * q[1] + p[2] * q[2]
    scalar = zero * (1.0 - 1.5 * dot(u, u)) + 3.0 * dot(one, u) + 4.5 * dot(bent, u)
    vector = [3.0 * (one[a] + 3.0 * bent[a] - zero * u[a]) for a in range(3)]
    start = rate * (scalar - dot(vector, u))
    slope = [(rate * factor) * v for v in vector]
    result = []
    for i in range(Q):
        lean = along(i, slope)
        relaxed = keep * m[i] + (start if lean is None else start + lean)
        result.append(jnp.where(wall, m[OPPOSITE[i]], relaxed))
    gradient = jnp.where(wall, 0.0, rate * density * dot(vector, plain))
    return result, gradient


def whole(shape):
    return pl.BlockSpec(shape, lambda *_: (0,) * len(shape))


def anywhere():
    return pl.BlockSpec(memory_space=pl.ANY)


def call(body, outs, ins, specs, scratch=(), flops=1, name=None):
    size = sum(math.prod(o) for o in outs) * 4 + sum(math.prod(x.shape) for x in ins) * 4
    return pl.pallas_call(
        body,
        out_shape=[jax.ShapeDtypeStruct(o, F32) for o in outs],
        grid=(1,),
        in_specs=specs,
        out_specs=[whole(o) for o in outs],
        scratch_shapes=list(scratch),
        cost_estimate=pl.CostEstimate(flops=flops, bytes_accessed=size, transcendentals=0),
        compiler_params=pltpu.CompilerParams(vmem_limit_bytes=40 * 1024 * 1024),
        name=name,
    )(*ins)


def edge_message(out, fill, design, node, p, later, up, down):
    density, momenta = moments(p)
    wall = node == 2.0
    for j in range(RAD + 1):
        fill(out, j, design[j])
    fill(out, NODE, node)
    fill(out, DENS, density)
    for a in range(3):
        fill(out, DENS + 1 + a, momenta[a])
    for k, i in enumerate(up):
        fill(out, FWD + k, jnp.where(wall, p[OPPOSITE[i]], p[i]))
    for k, i in enumerate(down):
        fill(out, ADJ + k, later(i))


def first_x_body(fwd_lo, fwd_hi, later_lo, later_hi, des_lo, des_hi, node_lo, node_hi, up_out, down_out):
    for out, fwd, later, des, node, up, down in (
        (up_out, fwd_hi, later_hi, des_hi, node_hi, XP, XM),
        (down_out, fwd_lo, later_lo, des_lo, node_lo, XM, XP),
    ):
        for h in (0, 8):
            rows = slice(h, h + 8)

            def fill(out, k, value, rows=rows):
                out[k, rows, :] = value

            edge_message(
                out,
                fill,
                [des[j, rows, :] for j in range(RAD + 1)],
                node[0, rows, :].astype(F32),
                [fwd[i, 0, rows, :] for i in range(Q)],
                lambda i, later=later, rows=rows: later[i, 0, rows, :],
                up,
                down,
            )


def first_x(fwd, later, design, node):
    def plane(at):
        return pl.BlockSpec((Q, 1, BY, NZ), lambda g: (0, at, 0, 0))

    def slab(depth, at):
        return pl.BlockSpec((depth, BY, NZ), lambda g: (at, 0, 0))

    return call(
        first_x_body,
        [(MSG, BY, NZ)] * 2,
        (fwd, fwd, later, later, design, design, node, node),
        [plane(0), plane(BX - 1), plane(0), plane(BX - 1), slab(4, 0), slab(4, 1), slab(1, 0), slab(1, BX - 1)],
        flops=200000,
        name="first_x",
    )


def first_y_body(fwd, later, design, node, up_out, down_out):
    for out, row, rows, up, down in (
        (up_out, BY - 1, range(BY - 4, BY), YP, YM),
        (down_out, 0, range(4), YM, YP),
    ):

        def fill(out, k, value):
            out[k] = value

        edge_message(
            out,
            fill,
            [design[:, j, :] for j in rows],
            node[:, row, :].astype(F32),
            [fwd[i, :, row, :] for i in range(Q)],
            lambda i, row=row: later[i, :, row, :],
            up,
            down,
        )


def first_y(fwd, later, design, node):
    ins = (fwd, later, design, node)
    return call(
        first_y_body, [(MSG, BX, NZ)] * 2, ins, [whole(x.shape) for x in ins], flops=400000, name="first_y"
    )


def join_y_body(own_up, own_down, low, high, up_out, down_out):
    for out, own, row, rows, up, down in (
        (up_out, own_up, BY - 1, range(BY - 4, BY), YP, YM),
        (down_out, own_down, 0, range(4), YM, YP),
    ):
        out[...] = jnp.zeros_like(out)
        for k, j in enumerate(rows):
            out[k, 4:12, :] = own[k]
            for x in range(4):
                out[k, x : x + 1, :] = low[x, j : j + 1, :]
                out[k, 12 + x : 13 + x, :] = high[x, j : j + 1, :]
        for k in range(NODE, MSG):
            out[k, 1:9, :] = own[k]
        for k in range(NODE, FWD):
            out[k, 0:1, :] = low[k, row : row + 1, :]
            out[k, 9:10, :] = high[k, row : row + 1, :]
        for first, mine, from_low, from_high in ((FWD, up, XP, XM), (ADJ, down, XM, XP)):
            for k, i in enumerate(mine):
                if i in from_low:
                    out[first + k, 0:1, :] = low[first + from_low.index(i), row : row + 1, :]
                if i in from_high:
                    out[first + k, 9:10, :] = high[first + from_high.index(i), row : row + 1, :]


def join_y(own_up, own_down, low, high):
    ins = (own_up, own_down, low, high)
    return call(
        join_y_body, [(MSG, BY, NZ)] * 2, ins, [whole(x.shape) for x in ins], flops=40000, name="join_y"
    )


ROW = 8
PADY = 32


def main_body(
    fwd, later_any, design, node, region, xlow, xhigh, ylow, yhigh,
    mid, flow, first, factor_out, part, up_out, down_out,
    wide, kinds, fine, post, later, sem,
):
    copy = pltpu.make_async_copy(later_any, later.at[:, 1 : 1 + BX, ROW : ROW + BY, :], sem)
    copy.start()
    wide[...] = jnp.zeros_like(wide)
    wide[4:12, ROW : ROW + BY, :] = design[...]
    wide[0:4, ROW : ROW + BY, :] = xlow[0:4]
    wide[12:16, ROW : ROW + BY, :] = xhigh[0:4]
    kinds[...] = jnp.zeros_like(kinds)
    kinds[1:9, ROW : ROW + BY, :] = node[...].astype(F32)
    kinds[0, ROW : ROW + BY, :] = xlow[NODE]
    kinds[9, ROW : ROW + BY, :] = xhigh[NODE]
    for x in range(16):
        for j in range(4):
            wide[x, ROW - 4 + j : ROW - 3 + j, :] = ylow[j, x : x + 1, :]
            wide[x, ROW + BY + j : ROW + BY + 1 + j, :] = yhigh[j, x : x + 1, :]
    for x in range(10):
        kinds[x, ROW - 1 : ROW, :] = ylow[NODE, x : x + 1, :]
        kinds[x, ROW + BY : ROW + BY + 1, :] = yhigh[NODE, x : x + 1, :]
    norm = norm_row((8, NZ))
    inverse_norm = 1.0 / norm

    def filter_plane(x, carry):
        for r in (4, 12, 20):
            value = filter_rows(lambda a, b: wide[x + RAD + a, r + b : r + b + 8, :]) * inverse_norm
            fine[x, r : r + 8, :] = value
        return carry

    lax.fori_loop(0, 10, filter_plane, 0)

    def factor_of(kind, filtered):
        return jnp.where(kind == 1.0, 1.0 - BRINKMAN * (1.0 - filtered), 1.0)

    for x, message, comps in ((0, xlow, XP), (9, xhigh, XM)):
        for h in (0, 8):
            rows = slice(h, h + 8)
            padded = slice(ROW + h, ROW + h + 8)
            kind = kinds[x, padded, :]
            q = {i: message[FWD + k, rows, :] for k, i in enumerate(comps)}
            value = post_tiles(
                comps, q, q, message[DENS, rows, :], [message[DENS + 1 + a, rows, :] for a in range(3)],
                kind, factor_of(kind, fine[x, padded, :]),
            )
            for i in comps:
                post[i, x, padded, :] = value[i]
    for row, message, comps in ((ROW - 1, ylow, YP), (ROW + BY, yhigh, YM)):
        kind = kinds[:, row, :]
        q = {i: message[FWD + k, 0:10, :] for k, i in enumerate(comps)}
        value = post_tiles(
            comps, q, q, message[DENS, 0:10, :], [message[DENS + 1 + a, 0:10, :] for a in range(3)],
            kind, factor_of(kind, fine[:, row, :]),
        )
        for i in comps:
            for x in range(10):
                post[i, x, row : row + 1, :] = value[i][x : x + 1, :]

    def post_plane(x, carry):
        carry = list(carry)
        for h in (0, 8):
            rows = slice(h, h + 8)
            padded = slice(ROW + h, ROW + h + 8)
            p = [fwd[i, x, rows, :] for i in range(Q)]
            density, momenta = moments(p)
            kind = kinds[x + 1, padded, :]
            filtered = fine[x + 1, padded, :]
            factor = factor_of(kind, filtered)
            factor_out[x, rows, :] = factor
            inverse = 1.0 / density
            flow[0, x, rows, :] = density
            for a in range(3):
                flow[1 + a, x, rows, :] = momenta[a] * inverse
            bounced = [p[OPPOSITE[i]] for i in range(Q)]
            value = post_tiles(range(Q), p, bounced, density, momenta, kind, factor)
            for i in range(Q):
                post[i, x + 1, padded, :] = value[i]
            counted = jnp.where(kind == 1.0, filtered, 0.0)
            where_region = region[x, rows, :]
            for r in range(REG):
                carry[r] = carry[r] + jnp.where(where_region == r, counted, 0.0)
        return tuple(carry)

    empty = jnp.zeros((8, NZ), F32)
    totals = lax.fori_loop(0, BX, post_plane, (empty,) * REG)
    for r in range(REG):
        part[r] = totals[r]

    copy.wait()
    for x, message, comps in ((0, xlow, XM), (9, xhigh, XP)):
        for k, i in enumerate(comps):
            later[i, x, ROW : ROW + BY, :] = message[ADJ + k]
    for row, message, comps in ((ROW - 1, ylow, YM), (ROW + BY, yhigh, YP)):
        for k, i in enumerate(comps):
            for x in range(10):
                later[i, x, row : row + 1, :] = message[ADJ + k, x : x + 1, :]

    def mid_plane(x, carry):
        for h in (0, 8):
            rows = slice(h, h + 8)
            padded = slice(ROW + h, ROW + h + 8)
            density, mx, my, mz = 0.0, 0.0, 0.0, 0.0
            for cz in (0, 1, -1):
                p = {}
                for i in range(Q):
                    if VELOCITY[i][2] == cz:
                        at = ROW + h - VELOCITY[i][1]
                        p[i] = post[i, x + 1 - VELOCITY[i][0], at : at + 8, :]
                whole_sum = shift_z(add_all(p.values()), -cz)
                density = density + whole_sum
                if cz:
                    mz = mz + cz * whole_sum
                sides = []
                for a in range(2):
                    up = add_all(p[i] for i in p if VELOCITY[i][a] == 1)
                    down = add_all(p[i] for i in p if VELOCITY[i][a] == -1)
                    sides.append(shift_z(up - down, -cz))
                mx = mx + sides[0]
                my = my + sides[1]
            kind = kinds[x + 1, padded, :]
            outlet = kind == 4.0
            carry = carry + jnp.where(outlet, mx, 0.0)
            inverse = 1.0 / density
            m = []
            for i in range(Q):
                at = ROW + h + VELOCITY[i][1]
                m.append(shift_z(later[i, x + 1 + VELOCITY[i][0], at : at + 8, :], VELOCITY[i][2]))
            value, gradient = back_tiles(
                m, density, [mx * inverse, my * inverse, mz * inverse], kind, factor_out[x, rows, :]
            )
            source = jnp.where(outlet, 1.0, 0.0)
            for i in range(Q):
                c = VELOCITY[i][0]
                mid[i, x, rows, :] = value[i] + c * source if c else value[i]
            first[x, rows, :] = gradient
        return carry

    part[REG] = lax.fori_loop(0, BX, mid_plane, empty)
    for k, i in enumerate(XM):
        up_out[k] = mid[i, BX - 1]
    for k, i in enumerate(XP):
        down_out[k] = mid[i, 0]


def main(fwd, later, design, node, region, xlow, xhigh, ylow, yhigh):
    ins = (fwd, later, design, node, region, xlow, xhigh, ylow, yhigh)
    specs = [whole(x.shape) for x in ins]
    specs[1] = anywhere()
    return call(
        main_body,
        [(Q, BX, BY, NZ), (4, BX, BY, NZ), (BX, BY, NZ), (BX, BY, NZ), (REG + 1, 8, NZ), (5, BY, NZ), (5, BY, NZ)],
        ins,
        specs,
        scratch=(
            pltpu.VMEM((16, PADY, NZ), F32),
            pltpu.VMEM((10, PADY, NZ), F32),
            pltpu.VMEM((10, PADY, NZ), F32),
            pltpu.VMEM((Q, 10, PADY, NZ), F32),
            pltpu.VMEM((Q, 10, PADY, NZ), F32),
            pltpu.SemaphoreType.DMA,
        ),
        flops=20000000,
        name="main",
    )


def mid_y_body(mid, low, high, up_out, down_out):
    for out, row, comps in ((up_out, BY - 1, YM), (down_out, 0, YP)):
        for k, i in enumerate(comps):
            out[k] = jnp.zeros((BY, NZ), F32)
            out[k, 1:9, :] = mid[i, :, row, :]
            if i in XM:
                out[k, 0:1, :] = low[XM.index(i), row : row + 1, :]
            if i in XP:
                out[k, 9:10, :] = high[XP.index(i), row : row + 1, :]


def mid_y(mid, low, high):
    ins = (mid, low, high)
    return call(mid_y_body, [(5, BY, NZ)] * 2, ins, [whole(x.shape) for x in ins], flops=20000, name="mid_y")


def last_body(mid_any, flow, first, factor, node, xlow, xhigh, ylow, yhigh, adjoint, raw, up_out, down_out, mid, sem):
    copy = pltpu.make_async_copy(mid_any, mid.at[:, 1 : 1 + BX, ROW : ROW + BY, :], sem)
    copy.start()
    for x, message, comps in ((0, xlow, XM), (9, xhigh, XP)):
        for k, i in enumerate(comps):
            mid[i, x, ROW : ROW + BY, :] = message[k]
    for row, message, comps in ((ROW - 1, ylow, YM), (ROW + BY, yhigh, YP)):
        for k, i in enumerate(comps):
            for x in range(10):
                mid[i, x, row : row + 1, :] = message[k, x : x + 1, :]
    inverse_norm = BRINKMAN / norm_row((8, NZ))
    copy.wait()

    def plane(x, carry):
        for h in (0, 8):
            rows = slice(h, h + 8)
            kind = node[x, rows, :].astype(F32)
            m = []
            for i in range(Q):
                at = ROW + h + VELOCITY[i][1]
                m.append(shift_z(mid[i, x + 1 + VELOCITY[i][0], at : at + 8, :], VELOCITY[i][2]))
            value, gradient = back_tiles(
                m, flow[0, x, rows, :], [flow[1 + a, x, rows, :] for a in range(3)], kind, factor[x, rows, :]
            )
            for i in range(Q):
                adjoint[i, x, rows, :] = value[i]
            both = (first[x, rows, :] + gradient) * inverse_norm
            raw[x, rows, :] = jnp.where(kind == 1.0, both, 0.0)
        return carry

    lax.fori_loop(0, BX, plane, 0)
    up_out[...] = raw[BX - RAD :]
    down_out[...] = raw[:RAD]


def last(mid, flow, first, factor, node, xlow, xhigh, ylow, yhigh):
    ins = (mid, flow, first, factor, node, xlow, xhigh, ylow, yhigh)
    specs = [whole(x.shape) for x in ins]
    specs[0] = anywhere()
    return call(
        last_body,
        [(Q, BX, BY, NZ), (BX, BY, NZ), (RAD, BY, NZ), (RAD, BY, NZ)],
        ins,
        specs,
        scratch=(pltpu.VMEM((Q, 10, PADY, NZ), F32), pltpu.SemaphoreType.DMA),
        flops=8000000,
        name="last",
    )


def raw_y_body(raw, low, high, up_out, down_out):
    for out, begin in ((up_out, BY - RAD), (down_out, 0)):
        out[...] = jnp.zeros_like(out)
        for j in range(RAD):
            out[j, RAD : RAD + BX, :] = raw[:, begin + j, :]
            for x in range(RAD):
                out[j, x : x + 1, :] = low[x, begin + j : begin + j + 1, :]
                out[j, RAD + BX + x : RAD + BX + x + 1, :] = high[x, begin + j : begin + j + 1, :]


def raw_y(raw, low, high):
    ins = (raw, low, high)
    return call(raw_y_body, [(RAD, BY, NZ)] * 2, ins, [whole(x.shape) for x in ins], flops=20000, name="raw_y")


def spread_body(raw, xlow, xhigh, ylow, yhigh, out, wide):
    wide[RAD : RAD + BX, ROW : ROW + BY, :] = raw[...]
    wide[0:RAD, ROW : ROW + BY, :] = xlow[...]
    wide[RAD + BX :, ROW : ROW + BY, :] = xhigh[...]
    for x in range(BX + 2 * RAD):
        for j in range(RAD):
            wide[x, ROW - RAD + j : ROW - RAD + j + 1, :] = ylow[j, x : x + 1, :]
            wide[x, ROW + BY + j : ROW + BY + j + 1, :] = yhigh[j, x : x + 1, :]

    def plane(x, carry):
        for h in (0, 8):
            at = ROW + h
            out[x, h : h + 8, :] = filter_rows(lambda a, b: wide[x + RAD + a, at + b : at + b + 8, :])
        return carry

    lax.fori_loop(0, BX, plane, 0)


def spread(raw, xlow, xhigh, ylow, yhigh):
    ins = (raw, xlow, xhigh, ylow, yhigh)
    return call(
        spread_body,
        [(BX, BY, NZ)],
        ins,
        [whole(x.shape) for x in ins],
        scratch=(pltpu.VMEM((BX + 2 * RAD, PADY, NZ), F32),),
        flops=2000000,
        name="spread",
    )[0]


def exchange(up, down, axis):
    count = lax.axis_size(axis)
    forward = [(i, (i + 1) % count) for i in range(count)]
    backward = [(j, i) for i, j in forward]
    return lax.ppermute(up, axis, forward), lax.ppermute(down, axis, backward)


def total(row):
    for axis in ("gy", "gx"):
        count = lax.axis_size(axis)
        rows = jnp.broadcast_to(row[None], (count,) + row.shape)
        row = jnp.sum(lax.all_to_all(rows, axis, 0, 0, tiled=True), axis=0)
    return row


def per_device(forward_pops, later_adjoint, design, node_type, region):
    up, down = first_x(forward_pops, later_adjoint, design, node_type)
    own_up, own_down = first_y(forward_pops, later_adjoint, design, node_type)
    xlow, xhigh = exchange(up, down, "gx")
    up, down = join_y(own_up, own_down, xlow, xhigh)
    ylow, yhigh = exchange(up, down, "gy")
    mid, flow, first, factor, part, up, down = main(
        forward_pops, later_adjoint, design, node_type, region, xlow, xhigh, ylow, yhigh
    )
    sums = total(jnp.pad(jnp.sum(part, axis=(1, 2)), (0, NZ - REG - 1)))
    xlow, xhigh = exchange(up, down, "gx")
    up, down = mid_y(mid, xlow, xhigh)
    ylow, yhigh = exchange(up, down, "gy")
    adjoint, raw, up, down = last(mid, flow, first, factor, node_type, xlow, xhigh, ylow, yhigh)
    xlow, xhigh = exchange(up, down, "gx")
    up, down = raw_y(raw, xlow, xhigh)
    ylow, yhigh = exchange(up, down, "gy")
    sensitivity = spread(raw, xlow, xhigh, ylow, yhigh)
    return adjoint, sensitivity, sums[REG], sums[:REG]


def solution(mesh):
    cells = P("gx", "gy", None)
    pops = P(None, "gx", "gy", None)
    return jax.shard_map(
        per_device,
        mesh=mesh,
        in_specs=(pops, pops, cells, cells, cells),
        out_specs=(pops, cells, P(), P()),
        check_vma=False,
    )
```

```python
import math

import jax
import jax.numpy as jnp
from jax import lax
from jax.experimental import pallas as pl
from jax.experimental.pallas import tpu as pltpu
from jax.sharding import PartitionSpec as P

RAD = 3
REG = 8
VELOCITY = [
    (0, 0, 0),
    (1, 0, 0),
    (-1, 0, 0),
    (0, 1, 0),
    (0, -1, 0),
    (0, 0, 1),
    (0, 0, -1),
    (1, 1, 0),
    (-1, -1, 0),
    (1, -1, 0),
    (-1, 1, 0),
    (1, 0, 1),
    (-1, 0, -1),
    (1, 0, -1),
    (-1, 0, 1),
    (0, 1, 1),
    (0, -1, -1),
    (0, 1, -1),
    (0, -1, 1),
]
WEIGHTS = [1.0 / 3.0] + [1.0 / 18.0] * 6 + [1.0 / 36.0] * 12
OPPOSITE = [0, 2, 1, 4, 3, 6, 5, 8, 7, 10, 9, 12, 11, 14, 13, 16, 15, 18, 17]
RELAXATION = 1.0 / 0.6
BRINKMAN = 0.9
Q = 19
BX = 8
BY = 16
NZ = 128
F32 = jnp.float32

XP = tuple(i for i in range(Q) if VELOCITY[i][0] == 1)
XM = tuple(i for i in range(Q) if VELOCITY[i][0] == -1)
YP = tuple(i for i in range(Q) if VELOCITY[i][1] == 1)
YM = tuple(i for i in range(Q) if VELOCITY[i][1] == -1)

KIND, DENS, MOVING = 0, 1, 5
DEEP = RAD + 2


def sided(axis, sign, ring):
    keep = (lambda c: c >= 0) if ring == 0 else (lambda c: c > 0)
    go = [i for i in range(Q) if keep(sign * VELOCITY[i][axis])]
    come = [i for i in range(Q) if keep(-sign * VELOCITY[i][axis])]
    return go, come


SIZES = [MOVING + sum(map(len, sided(0, 1, ring))) for ring in (0, 1)]
BASES = (0, SIZES[0])
DESIGN = sum(SIZES)
MSG = DESIGN + DEEP
WIDE_ROWS = 24
FLAT = DESIGN * BY + DEEP * WIDE_ROWS


def slot(axis, sign, ring, field, which=None):
    base = BASES[ring]
    if field in ("go", "come"):
        go, come = sided(axis, sign, ring)
        listed = go if field == "go" else come
        if which not in listed:
            return None
        return base + MOVING + (0 if field == "go" else len(go)) + listed.index(which)
    return base + field


CLASSES = sorted(
    {a * a + b * b for a in range(RAD + 1) for b in range(RAD + 1) if a * a + b * b < (RAD + 1) ** 2}
)
TAPS = {
    s: [
        (a, b)
        for a in range(-RAD, RAD + 1)
        for b in range(-RAD, RAD + 1)
        if a * a + b * b == s
    ]
    for s in CLASSES
}


def tap_weight(s, c):
    return RAD + 1 - math.sqrt(s + c * c)


def lanes(shape):
    return lax.broadcasted_iota(jnp.int32, shape, len(shape) - 1)


def shift_z(value, c):
    if c == 0:
        return value
    z = lanes(value.shape)
    moved = pltpu.roll(value, (-c) % NZ, value.ndim - 1)
    return jnp.where((z + c >= 0) & (z + c < NZ), moved, 0.0)


def norm_row(shape):
    z = lanes(shape)
    result = None
    for c in range(RAD + 1):
        total = sum(len(TAPS[s]) * tap_weight(s, c) for s in CLASSES if tap_weight(s, c) > 0)
        if c == 0:
            result = jnp.full(shape, total, F32)
        else:
            result = result + jnp.where(z >= c, total, 0.0) + jnp.where(z < NZ - c, total, 0.0)
    return result


def filter_rows(load):
    sums = []
    for s in CLASSES:
        running = None
        for a, b in TAPS[s]:
            tile = load(a, b)
            running = tile if running is None else running + tile
        sums.append(running)
    result = None
    for c in range(RAD + 1):
        mixed = None
        for s, part in zip(CLASSES, sums):
            if tap_weight(s, c) > 0:
                term = tap_weight(s, c) * part
                mixed = term if mixed is None else mixed + term
        if c == 0:
            result = mixed
        else:
            result = result + shift_z(mixed, c) + shift_z(mixed, -c)
    return result


def add_all(values):
    values = list(values)
    while len(values) > 1:
        values = [
            values[k] + values[k + 1] if k + 1 < len(values) else values[k]
            for k in range(0, len(values), 2)
        ]
    return values[0]


def moments(p):
    momenta = []
    for a in range(3):
        up = add_all(p[i] for i in range(Q) if VELOCITY[i][a] == 1)
        down = add_all(p[i] for i in range(Q) if VELOCITY[i][a] == -1)
        momenta.append(up - down)
    return add_all(p), momenta


def along(i, vector):
    result = None
    for a in range(3):
        c = VELOCITY[i][a]
        if c == 0:
            continue
        if result is None:
            result = vector[a] if c == 1 else -vector[a]
        else:
            result = result + vector[a] if c == 1 else result - vector[a]
    return result


def post_tiles(which, straight, bounced, density, momenta, node, factor):
    inverse = 1.0 / density
    u = [factor * (m * inverse) for m in momenta]
    rest = 1.0 - 1.5 * (u[0] * u[0] + u[1] * u[1] + u[2] * u[2])
    rate = jnp.where(node <= 1.5, RELAXATION, 1.0)
    keep = 1.0 - rate
    wall = node == 2.0
    scale = rate * density
    result = {}
    for i in which:
        a = along(i, u)
        form = rest if a is None else rest + a * (3.0 + 4.5 * a)
        relaxed = keep * straight[i] + (WEIGHTS[i] * scale) * form
        result[i] = jnp.where(wall, bounced[i], relaxed)
    return result


def back_tiles(m, density, plain, node, factor):
    u = [factor * q for q in plain]
    rate = jnp.where(node <= 1.5, RELAXATION, 1.0)
    keep = 1.0 - rate
    wall = node == 2.0

    def weighted(select):
        total = None
        for w, group in ((1.0 / 18.0, range(1, 7)), (1.0 / 36.0, range(7, Q))):
            up = [m[i] for i in group if select(VELOCITY[i]) > 0]
            down = [m[i] for i in group if select(VELOCITY[i]) < 0]
            if not up and not down:
                continue
            value = add_all(up)
            if down:
                value = value - add_all(down)
            value = w * value
            total = value if total is None else total + value
        return total

    zero = (1.0 / 3.0) * m[0] + weighted(lambda c: 1)
    one = [weighted(lambda c, a=a: c[a]) for a in range(3)]
    two = {}
    for a in range(3):
        for b in range(a, 3):
            two[a, b] = two[b, a] = weighted(lambda c, a=a, b=b: c[a] * c[b])
    bent = [two[a, 0] * u[0] + two[a, 1] * u[1] + two[a, 2] * u[2] for a in range(3)]
    dot = lambda p, q: p[0] * q[0] + p[1] * q[1] + p[2] * q[2]
    scalar = zero * (1.0 - 1.5 * dot(u, u)) + 3.0 * dot(one, u) + 4.5 * dot(bent, u)
    vector = [3.0 * (one[a] + 3.0 * bent[a] - zero * u[a]) for a in range(3)]
    start = rate * (scalar - dot(vector, u))
    slope = [(rate * factor) * v for v in vector]
    result = []
    for i in range(Q):
        lean = along(i, slope)
        relaxed = keep * m[i] + (start if lean is None else start + lean)
        result.append(jnp.where(wall, m[OPPOSITE[i]], relaxed))
    gradient = jnp.where(wall, 0.0, rate * density * dot(vector, plain))
    return result, gradient


def whole(shape):
    return pl.BlockSpec(shape, lambda *_: (0,) * len(shape))


def scalar():
    return pl.BlockSpec(memory_space=pltpu.SMEM)


def anywhere():
    return pl.BlockSpec(memory_space=pl.ANY)


def call(body, outs, ins, specs, scratch=(), flops=1, name=None):
    size = sum(math.prod(o) for o in outs) * 4 + sum(math.prod(x.shape) for x in ins) * 4
    return pl.pallas_call(
        body,
        out_shape=[jax.ShapeDtypeStruct(o, F32) for o in outs],
        grid=(1,),
        in_specs=specs,
        out_specs=[whole(o) for o in outs],
        scratch_shapes=list(scratch),
        cost_estimate=pl.CostEstimate(flops=flops, bytes_accessed=size, transcendentals=0),
        compiler_params=pltpu.CompilerParams(vmem_limit_bytes=40 * 1024 * 1024),
        name=name,
    )(*ins)


def ring_fields(axis, sign, ring, p, node, later):
    density, momenta = moments(p)
    wall = node == 2.0
    go, come = sided(axis, sign, ring)
    fields = [node, density, *momenta]
    fields += [jnp.where(wall, p[OPPOSITE[i]], p[i]) for i in go]
    return fields + [later(i) for i in come]


def first_x_body(fwd_any, later_any, des, node, up_out, down_out, fwd, later, sems):
    copies = []
    for k, (source, target) in enumerate(((fwd_any, fwd), (later_any, later))):
        for e in (0, 1):
            copies.append(
                pltpu.make_async_copy(
                    source.at[:, e * (BX - 2) : e * (BX - 2) + 2], target.at[:, 2 * e : 2 * e + 2], sems.at[k, e]
                )
            )
    for copy in copies:
        copy.start()
    up_out[DESIGN:] = des[BX - DEEP :]
    down_out[DESIGN:] = des[:DEEP]
    for copy in copies:
        copy.wait()
    for out, sign, planes in ((up_out, 1, (BX - 1, BX - 2)), (down_out, -1, (0, 1))):
        for ring, x in enumerate(planes):
            at = x if x < 2 else x - (BX - 4)
            for h in (0, 8):
                rows = slice(h, h + 8)
                fields = ring_fields(
                    0,
                    sign,
                    ring,
                    [fwd[i, at, rows, :] for i in range(Q)],
                    node[x, rows, :].astype(F32),
                    lambda i, at=at, rows=rows: later[i, at, rows, :],
                )
                for k, value in enumerate(fields):
                    out[BASES[ring] + k, rows, :] = value


def first_x(fwd, later, design, node):
    return call(
        first_x_body,
        [(MSG, BY, NZ)] * 2,
        (fwd, later, design, node),
        [pl.BlockSpec(memory_space=pltpu.HBM)] * 2 + [whole(design.shape), whole(node.shape)],
        scratch=(
            pltpu.VMEM((Q, 4, BY, NZ), F32),
            pltpu.VMEM((Q, 4, BY, NZ), F32),
            pltpu.SemaphoreType.DMA((2, 2)),
        ),
        flops=400000,
        name="first_x",
    )


def first_y_body(fwd, later, design, node, up_out, down_out):
    for out, sign, lines, deep in (
        (up_out, 1, (BY - 1, BY - 2), range(BY - DEEP, BY)),
        (down_out, -1, (0, 1), range(DEEP)),
    ):
        for k, y in enumerate(deep):
            out[DESIGN + k] = design[:, y, :]
        for ring, y in enumerate(lines):
            fields = ring_fields(
                1,
                sign,
                ring,
                [fwd[i, :, y, :] for i in range(Q)],
                node[:, y, :].astype(F32),
                lambda i, y=y: later[i, :, y, :],
            )
            for k, value in enumerate(fields):
                out[BASES[ring] + k] = value


def first_y(fwd, later, design, node):
    ins = (fwd, later, design, node)
    return call(
        first_y_body, [(MSG, BX, NZ)] * 2, ins, [whole(x.shape) for x in ins], flops=800000, name="first_y"
    )


def by_parity(odd, up, down, near_out, far_out):
    @pl.when(odd[0] == 0)
    def _():
        near_out[...] = up[...]
        far_out[...] = down[...]

    @pl.when(odd[0] == 1)
    def _():
        near_out[...] = down[...]
        far_out[...] = up[...]


def to_sides(odd, near, far, low, high):
    @pl.when(odd[0] == 0)
    def _():
        high[...] = near[...]
        low[...] = far[...]

    @pl.when(odd[0] == 1)
    def _():
        low[...] = near[...]
        high[...] = far[...]


def join_y_body(odd, own_up, own_down, low, high, near_out, far_out, up_out, down_out):
    for out, own, sign, lines, deep in (
        (up_out, own_up, 1, (BY - 1, BY - 2), range(BY - DEEP, BY)),
        (down_out, own_down, -1, (0, 1), range(DEEP)),
    ):
        out[...] = jnp.zeros_like(out)
        for k, y in enumerate(deep):
            base = DESIGN * BY + k * WIDE_ROWS
            out[base + DEEP : base + DEEP + BX, :] = own[DESIGN + k]
            for x in range(DEEP):
                out[base + x : base + x + 1, :] = low[DESIGN + x, y : y + 1, :]
                at = base + DEEP + BX + x
                out[at : at + 1, :] = high[DESIGN + x, y : y + 1, :]
        for ring, y in enumerate(lines):
            go, come = sided(1, sign, ring)
            fields = [(f, None) for f in range(MOVING)] + [("go", i) for i in go] + [("come", i) for i in come]
            for k, (field, i) in enumerate(fields):
                base = (BASES[ring] + k) * BY
                out[base + 2 : base + 2 + BX, :] = own[BASES[ring] + k]
                for source, side, places in ((low, 1, (1, 0)), (high, -1, (2 + BX, 3 + BX))):
                    for other in (0, 1):
                        found = slot(0, side, other, field, i)
                        if found is not None:
                            at = base + places[other]
                            out[at : at + 1, :] = source[found, y : y + 1, :]
    by_parity(odd, up_out, down_out, near_out, far_out)


def join_y(odd, own_up, own_down, low, high):
    ins = (odd, own_up, own_down, low, high)
    return call(
        join_y_body,
        [(FLAT, NZ)] * 2,
        ins,
        [scalar()] + [whole(x.shape) for x in ins[1:]],
        scratch=(pltpu.VMEM((FLAT, NZ), F32),) * 2,
        flops=80000,
        name="join_y",
    )


EX = BX + 4
ROW = 8
PADY = 32


def main_body(
    odd, fwd, later_any, design, node, region, xlow, xhigh, near, far,
    adjoint, raw, part, up_out, down_out,
    ylow, yhigh, wide, kinds, fine, post, later, mid, flow, flux, first, sem,
):
    copy = pltpu.make_async_copy(later_any, later.at[:, 2 : 2 + BX, ROW : ROW + BY, :], sem)
    copy.start()
    to_sides(odd, near, far, ylow, yhigh)
    wide[...] = jnp.zeros_like(wide)
    wide[DEEP : DEEP + BX, ROW : ROW + BY, :] = design[...]
    wide[0:DEEP, ROW : ROW + BY, :] = xlow[DESIGN:]
    wide[DEEP + BX :, ROW : ROW + BY, :] = xhigh[DESIGN:]
    for j in range(DEEP):
        for x in range(BX + 2 * DEEP):
            at = DESIGN * BY + j * WIDE_ROWS + x
            wide[x, ROW - DEEP + j : ROW - DEEP + j + 1, :] = ylow[at : at + 1, :]
            wide[x, ROW + BY + j : ROW + BY + j + 1, :] = yhigh[at : at + 1, :]
    xrings = ((1, xlow, 1, 0), (0, xlow, 1, 1), (2 + BX, xhigh, -1, 0), (3 + BX, xhigh, -1, 1))
    yrings = ((ROW - 1, ylow, 1, 0), (ROW - 2, ylow, 1, 1), (ROW + BY, yhigh, -1, 0), (ROW + BY + 1, yhigh, -1, 1))
    kinds[...] = jnp.zeros_like(kinds)
    kinds[2 : 2 + BX, ROW : ROW + BY, :] = node[...].astype(F32)
    for x, message, sign, ring in xrings:
        kinds[x, ROW : ROW + BY, :] = message[slot(0, sign, ring, KIND)]
    for row, message, sign, ring in yrings:
        base = slot(1, sign, ring, KIND) * BY
        for x in range(EX):
            kinds[x, row : row + 1, :] = message[base + x : base + x + 1, :]
    inverse_norm = 1.0 / norm_row((8, NZ))

    def filter_plane(x, carry):
        for r in (4, 12, 20):
            value = filter_rows(lambda a, b: wide[x + RAD + a, r + b : r + b + 8, :]) * inverse_norm
            fine[x, r : r + 8, :] = value
        return carry

    lax.fori_loop(0, EX, filter_plane, 0)

    def factor_of(kind, filtered):
        return jnp.where(kind == 1.0, 1.0 - BRINKMAN * (1.0 - filtered), 1.0)

    for x, message, sign, ring in xrings:
        comps = sided(0, sign, ring)[0]
        for h in (0, 8):
            rows = slice(h, h + 8)
            padded = slice(ROW + h, ROW + h + 8)
            kind = kinds[x, padded, :]
            q = {i: message[slot(0, sign, ring, "go", i), rows, :] for i in comps}
            base = slot(0, sign, ring, DENS)
            value = post_tiles(
                comps, q, q, message[base, rows, :], [message[base + 1 + a, rows, :] for a in range(3)],
                kind, factor_of(kind, fine[x, padded, :]),
            )
            for i in comps:
                post[i, x, padded, :] = value[i]
    for row, message, sign, ring in yrings:
        comps = sided(1, sign, ring)[0]
        kind = kinds[:, row, :]

        def line(k, message=message):
            return message[k * BY : k * BY + EX, :]

        q = {i: line(slot(1, sign, ring, "go", i)) for i in comps}
        base = slot(1, sign, ring, DENS)
        value = post_tiles(
            comps, q, q, line(base), [line(base + 1 + a) for a in range(3)],
            kind, factor_of(kind, fine[:, row, :]),
        )
        for i in comps:
            for x in range(EX):
                post[i, x, row : row + 1, :] = value[i][x : x + 1, :]

    def post_plane(x, carry):
        carry = list(carry)
        for h in (0, 8):
            rows = slice(h, h + 8)
            padded = slice(ROW + h, ROW + h + 8)
            p = [fwd[i, x, rows, :] for i in range(Q)]
            density, momenta = moments(p)
            kind = kinds[x + 2, padded, :]
            filtered = fine[x + 2, padded, :]
            inverse = 1.0 / density
            flow[0, x, rows, :] = density
            for a in range(3):
                flow[1 + a, x, rows, :] = momenta[a] * inverse
            bounced = [p[OPPOSITE[i]] for i in range(Q)]
            value = post_tiles(range(Q), p, bounced, density, momenta, kind, factor_of(kind, filtered))
            for i in range(Q):
                post[i, x + 2, padded, :] = value[i]
            counted = jnp.where(kind == 1.0, filtered, 0.0)
            where_region = region[x, rows, :]
            for r in range(REG):
                carry[r] = carry[r] + jnp.where(where_region == r, counted, 0.0)
        return tuple(carry)

    empty = jnp.zeros((8, NZ), F32)
    totals = lax.fori_loop(0, BX, post_plane, (empty,) * REG)
    for r in range(REG):
        part[r] = totals[r]

    copy.wait()
    for x, message, sign, ring in xrings:
        for i in sided(0, sign, ring)[1]:
            later[i, x, ROW : ROW + BY, :] = message[slot(0, sign, ring, "come", i)]
    for row, message, sign, ring in yrings:
        for i in sided(1, sign, ring)[1]:
            base = slot(1, sign, ring, "come", i) * BY
            for x in range(EX):
                later[i, x, row : row + 1, :] = message[base + x : base + x + 1, :]

    def mid_plane(x, carry):
        for start in (ROW - 1, ROW + 7, ROW + 15):
            rows = slice(start, start + 8)
            density, mx, my, mz = 0.0, 0.0, 0.0, 0.0
            for cz in (0, 1, -1):
                p = {}
                for i in range(Q):
                    if VELOCITY[i][2] == cz:
                        at = start - VELOCITY[i][1]
                        p[i] = post[i, x + 1 - VELOCITY[i][0], at : at + 8, :]
                whole_sum = shift_z(add_all(p.values()), -cz)
                density = density + whole_sum
                if cz:
                    mz = mz + cz * whole_sum
                sides = []
                for a in range(2):
                    up = add_all(p[i] for i in p if VELOCITY[i][a] == 1)
                    down = add_all(p[i] for i in p if VELOCITY[i][a] == -1)
                    sides.append(shift_z(up - down, -cz))
                mx = mx + sides[0]
                my = my + sides[1]
            kind = kinds[x + 1, rows, :]
            outlet = kind == 4.0
            flux[x, rows, :] = jnp.where(outlet, mx, 0.0)
            inverse = 1.0 / density
            m = []
            for i in range(Q):
                at = start + VELOCITY[i][1]
                m.append(shift_z(later[i, x + 1 + VELOCITY[i][0], at : at + 8, :], VELOCITY[i][2]))
            value, gradient = back_tiles(
                m, density, [mx * inverse, my * inverse, mz * inverse], kind,
                factor_of(kind, fine[x + 1, rows, :]),
            )
            source = jnp.where(outlet, 1.0, 0.0)
            for i in range(Q):
                c = VELOCITY[i][0]
                mid[i, x, rows, :] = value[i] + c * source if c else value[i]
            first[x, rows, :] = gradient
        return carry

    lax.fori_loop(0, BX + 2, mid_plane, 0)
    raw_scale = BRINKMAN * inverse_norm

    def last_plane(x, carry):
        for h in (0, 8):
            rows = slice(h, h + 8)
            padded = slice(ROW + h, ROW + h + 8)
            kind = kinds[x + 2, padded, :]
            carry = carry + flux[x + 1, padded, :]
            m = []
            for i in range(Q):
                at = ROW + h + VELOCITY[i][1]
                m.append(shift_z(mid[i, x + 1 + VELOCITY[i][0], at : at + 8, :], VELOCITY[i][2]))
            value, gradient = back_tiles(
                m, flow[0, x, rows, :], [flow[1 + a, x, rows, :] for a in range(3)], kind,
                factor_of(kind, fine[x + 2, padded, :]),
            )
            for i in range(Q):
                adjoint[i, x, rows, :] = value[i]
            both = (first[x + 1, padded, :] + gradient) * raw_scale
            raw[x, rows, :] = jnp.where(kind == 1.0, both, 0.0)
        return carry

    part[REG] = lax.fori_loop(0, BX, last_plane, empty)
    up_out[...] = raw[BX - RAD :]
    down_out[...] = raw[:RAD]


def main(odd, fwd, later, design, node, region, xlow, xhigh, near, far):
    ins = (odd, fwd, later, design, node, region, xlow, xhigh, near, far)
    specs = [scalar()] + [whole(x.shape) for x in ins[1:]]
    specs[2] = anywhere()
    return call(
        main_body,
        [(Q, BX, BY, NZ), (BX, BY, NZ), (REG + 1, 8, NZ), (RAD, BY, NZ), (RAD, BY, NZ)],
        ins,
        specs,
        scratch=(
            pltpu.VMEM((FLAT, NZ), F32),
            pltpu.VMEM((FLAT, NZ), F32),
            pltpu.VMEM((BX + 2 * DEEP, PADY, NZ), F32),
            pltpu.VMEM((EX, PADY, NZ), F32),
            pltpu.VMEM((EX, PADY, NZ), F32),
            pltpu.VMEM((Q, EX, PADY, NZ), F32),
            pltpu.VMEM((Q, EX, PADY, NZ), F32),
            pltpu.VMEM((Q, BX + 2, PADY, NZ), F32),
            pltpu.VMEM((4, BX, BY, NZ), F32),
            pltpu.VMEM((BX + 2, PADY, NZ), F32),
            pltpu.VMEM((BX + 2, PADY, NZ), F32),
            pltpu.SemaphoreType.DMA,
        ),
        flops=30000000,
        name="main",
    )


def raw_y_body(odd, raw, low, high, near_out, far_out, up_out, down_out):
    for out, begin in ((up_out, BY - RAD), (down_out, 0)):
        out[...] = jnp.zeros_like(out)
        for j in range(RAD):
            out[j, RAD : RAD + BX, :] = raw[:, begin + j, :]
            for x in range(RAD):
                out[j, x : x + 1, :] = low[x, begin + j : begin + j + 1, :]
                out[j, RAD + BX + x : RAD + BX + x + 1, :] = high[x, begin + j : begin + j + 1, :]
    by_parity(odd, up_out, down_out, near_out, far_out)


def raw_y(odd, raw, low, high):
    ins = (odd, raw, low, high)
    return call(
        raw_y_body,
        [(RAD, BY, NZ)] * 2,
        ins,
        [scalar()] + [whole(x.shape) for x in ins[1:]],
        scratch=(pltpu.VMEM((RAD, BY, NZ), F32),) * 2,
        flops=20000,
        name="raw_y",
    )


def spread_body(odd, raw, xlow, xhigh, near, far, out, ylow, yhigh, wide):
    to_sides(odd, near, far, ylow, yhigh)
    wide[RAD : RAD + BX, ROW : ROW + BY, :] = raw[...]
    wide[0:RAD, ROW : ROW + BY, :] = xlow[...]
    wide[RAD + BX :, ROW : ROW + BY, :] = xhigh[...]
    for x in range(BX + 2 * RAD):
        for j in range(RAD):
            wide[x, ROW - RAD + j : ROW - RAD + j + 1, :] = ylow[j, x : x + 1, :]
            wide[x, ROW + BY + j : ROW + BY + j + 1, :] = yhigh[j, x : x + 1, :]

    def plane(x, carry):
        for h in (0, 8):
            at = ROW + h
            out[x, h : h + 8, :] = filter_rows(lambda a, b: wide[x + RAD + a, at + b : at + b + 8, :])
        return carry

    lax.fori_loop(0, BX, plane, 0)


def spread(odd, raw, xlow, xhigh, near, far):
    ins = (odd, raw, xlow, xhigh, near, far)
    return call(
        spread_body,
        [(BX, BY, NZ)],
        ins,
        [scalar()] + [whole(x.shape) for x in ins[1:]],
        scratch=(pltpu.VMEM((RAD, BY, NZ), F32),) * 2 + (pltpu.VMEM((BX + 2 * RAD, PADY, NZ), F32),),
        flops=2000000,
        name="spread",
    )[0]


def exchange(up, down, axis):
    count = lax.axis_size(axis)
    forward = [(i, (i + 1) % count) for i in range(count)]
    backward = [(j, i) for i, j in forward]
    return lax.ppermute(up, axis, forward), lax.ppermute(down, axis, backward)


def swap(near, far, axis):
    count = lax.axis_size(axis)
    inner = [(i, i ^ 1) for i in range(count)]
    outer = [(i, (i + 1 if i % 2 else i - 1) % count) for i in range(count)]
    return lax.ppermute(near, axis, inner), lax.ppermute(far, axis, outer)


def total(row):
    axes = ("gx", "gy")
    count = lax.axis_size(axes)
    rows = jnp.broadcast_to(row[None], (count,) + row.shape)
    return jnp.sum(lax.all_to_all(rows, axes, 0, 0, tiled=True), axis=0)


def per_device(forward_pops, later_adjoint, design, node_type, region):
    odd = jnp.reshape(lax.axis_index("gy") % 2, (1,)).astype(jnp.int32)
    up, down = first_x(forward_pops, later_adjoint, design, node_type)
    own_up, own_down = first_y(forward_pops, later_adjoint, design, node_type)
    xlow, xhigh = exchange(up, down, "gx")
    near, far = swap(*join_y(odd, own_up, own_down, xlow, xhigh), "gy")
    adjoint, raw, part, up, down = main(
        odd, forward_pops, later_adjoint, design, node_type, region, xlow, xhigh, near, far
    )
    sums = total(jnp.pad(jnp.sum(part, axis=(1, 2)), (0, NZ - REG - 1)))
    xlow, xhigh = exchange(up, down, "gx")
    near, far = swap(*raw_y(odd, raw, xlow, xhigh), "gy")
    sensitivity = spread(odd, raw, xlow, xhigh, near, far)
    return adjoint, sensitivity, sums[REG], sums[:REG]


def solution(mesh):
    cells = P("gx", "gy", None)
    pops = P(None, "gx", "gy", None)
    return jax.shard_map(
        per_device,
        mesh=mesh,
        in_specs=(pops, pops, cells, cells, cells),
        out_specs=(pops, cells, P(), P()),
        check_vma=False,
    )
```

```python
import math

import jax
import jax.numpy as jnp
from jax import lax
from jax.experimental import pallas as pl
from jax.experimental.pallas import tpu as pltpu
from jax.sharding import PartitionSpec as P

RAD = 3
REG = 8
VELOCITY = [
    (0, 0, 0),
    (1, 0, 0),
    (-1, 0, 0),
    (0, 1, 0),
    (0, -1, 0),
    (0, 0, 1),
    (0, 0, -1),
    (1, 1, 0),
    (-1, -1, 0),
    (1, -1, 0),
    (-1, 1, 0),
    (1, 0, 1),
    (-1, 0, -1),
    (1, 0, -1),
    (-1, 0, 1),
    (0, 1, 1),
    (0, -1, -1),
    (0, 1, -1),
    (0, -1, 1),
]
WEIGHTS = [1.0 / 3.0] + [1.0 / 18.0] * 6 + [1.0 / 36.0] * 12
OPPOSITE = [0, 2, 1, 4, 3, 6, 5, 8, 7, 10, 9, 12, 11, 14, 13, 16, 15, 18, 17]
RELAXATION = 1.0 / 0.6
BRINKMAN = 0.9
Q = 19
BX = 8
BY = 16
NZ = 128
F32 = jnp.float32


KIND, DENS, MOVING = 0, 1, 5
DEEP = RAD + 2


def sided(axis, sign, ring):
    keep = (lambda c: c >= 0) if ring == 0 else (lambda c: c > 0)
    go = [i for i in range(Q) if keep(sign * VELOCITY[i][axis])]
    come = [i for i in range(Q) if keep(-sign * VELOCITY[i][axis])]
    return go, come


SIZES = [MOVING + sum(map(len, sided(0, 1, ring))) for ring in (0, 1)]
BASES = (0, SIZES[0])
DESIGN = sum(SIZES)
MSG = DESIGN + DEEP
LINE = BY + 4
WIDE_LINE = BY + 2 * DEEP
FLAT = (DESIGN * LINE + DEEP * WIDE_LINE + 7) // 8 * 8
RAW_ROWS = RAD * BY


def design_row(j):
    return DESIGN * LINE + j * WIDE_LINE


def slot(axis, sign, ring, field, which=None):
    base = BASES[ring]
    if field in ("go", "come"):
        go, come = sided(axis, sign, ring)
        listed = go if field == "go" else come
        if which not in listed:
            return None
        return base + MOVING + (0 if field == "go" else len(go)) + listed.index(which)
    return base + field


CLASSES = sorted(
    {a * a + b * b for a in range(RAD + 1) for b in range(RAD + 1) if a * a + b * b < (RAD + 1) ** 2}
)
TAPS = {
    s: [
        (a, b)
        for a in range(-RAD, RAD + 1)
        for b in range(-RAD, RAD + 1)
        if a * a + b * b == s
    ]
    for s in CLASSES
}


def tap_weight(s, c):
    return RAD + 1 - math.sqrt(s + c * c)


def lanes(shape):
    return lax.broadcasted_iota(jnp.int32, shape, len(shape) - 1)


def shift_z(value, c):
    if c == 0:
        return value
    z = lanes(value.shape)
    moved = pltpu.roll(value, (-c) % NZ, value.ndim - 1)
    return jnp.where((z + c >= 0) & (z + c < NZ), moved, 0.0)


def norm_row(shape):
    z = lanes(shape)
    result = None
    for c in range(RAD + 1):
        total = sum(len(TAPS[s]) * tap_weight(s, c) for s in CLASSES if tap_weight(s, c) > 0)
        if c == 0:
            result = jnp.full(shape, total, F32)
        else:
            result = result + jnp.where(z >= c, total, 0.0) + jnp.where(z < NZ - c, total, 0.0)
    return result


def filter_rows(load):
    sums = []
    for s in CLASSES:
        running = None
        for a, b in TAPS[s]:
            tile = load(a, b)
            running = tile if running is None else running + tile
        sums.append(running)
    result = None
    for c in range(RAD + 1):
        mixed = None
        for s, part in zip(CLASSES, sums):
            if tap_weight(s, c) > 0:
                term = tap_weight(s, c) * part
                mixed = term if mixed is None else mixed + term
        if c == 0:
            result = mixed
        else:
            result = result + shift_z(mixed, c) + shift_z(mixed, -c)
    return result


def add_all(values):
    values = list(values)
    while len(values) > 1:
        values = [
            values[k] + values[k + 1] if k + 1 < len(values) else values[k]
            for k in range(0, len(values), 2)
        ]
    return values[0]


def moments(p):
    momenta = []
    for a in range(3):
        up = add_all(p[i] for i in range(Q) if VELOCITY[i][a] == 1)
        down = add_all(p[i] for i in range(Q) if VELOCITY[i][a] == -1)
        momenta.append(up - down)
    return add_all(p), momenta


def along(i, vector):
    result = None
    for a in range(3):
        c = VELOCITY[i][a]
        if c == 0:
            continue
        if result is None:
            result = vector[a] if c == 1 else -vector[a]
        else:
            result = result + vector[a] if c == 1 else result - vector[a]
    return result


def post_tiles(which, straight, bounced, density, momenta, node, factor):
    inverse = 1.0 / density
    u = [factor * (m * inverse) for m in momenta]
    rest = 1.0 - 1.5 * (u[0] * u[0] + u[1] * u[1] + u[2] * u[2])
    rate = jnp.where(node <= 1.5, RELAXATION, 1.0)
    keep = 1.0 - rate
    wall = node == 2.0
    scale = rate * density
    result = {}
    for i in which:
        a = along(i, u)
        form = rest if a is None else rest + a * (3.0 + 4.5 * a)
        relaxed = keep * straight[i] + (WEIGHTS[i] * scale) * form
        result[i] = jnp.where(wall, bounced[i], relaxed)
    return result


def back_tiles(m, density, plain, node, factor):
    u = [factor * q for q in plain]
    rate = jnp.where(node <= 1.5, RELAXATION, 1.0)
    keep = 1.0 - rate
    wall = node == 2.0

    def weighted(select):
        total = None
        for w, group in ((1.0 / 18.0, range(1, 7)), (1.0 / 36.0, range(7, Q))):
            up = [m[i] for i in group if select(VELOCITY[i]) > 0]
            down = [m[i] for i in group if select(VELOCITY[i]) < 0]
            if not up and not down:
                continue
            value = add_all(up)
            if down:
                value = value - add_all(down)
            value = w * value
            total = value if total is None else total + value
        return total

    zero = (1.0 / 3.0) * m[0] + weighted(lambda c: 1)
    one = [weighted(lambda c, a=a: c[a]) for a in range(3)]
    two = {}
    for a in range(3):
        for b in range(a, 3):
            two[a, b] = two[b, a] = weighted(lambda c, a=a, b=b: c[a] * c[b])
    bent = [two[a, 0] * u[0] + two[a, 1] * u[1] + two[a, 2] * u[2] for a in range(3)]
    dot = lambda p, q: p[0] * q[0] + p[1] * q[1] + p[2] * q[2]
    scalar = zero * (1.0 - 1.5 * dot(u, u)) + 3.0 * dot(one, u) + 4.5 * dot(bent, u)
    vector = [3.0 * (one[a] + 3.0 * bent[a] - zero * u[a]) for a in range(3)]
    start = rate * (scalar - dot(vector, u))
    slope = [(rate * factor) * v for v in vector]
    result = []
    for i in range(Q):
        lean = along(i, slope)
        relaxed = keep * m[i] + (start if lean is None else start + lean)
        result.append(jnp.where(wall, m[OPPOSITE[i]], relaxed))
    gradient = jnp.where(wall, 0.0, rate * density * dot(vector, plain))
    return result, gradient


def whole(shape):
    return pl.BlockSpec(shape, lambda *_: (0,) * len(shape))


def scalar():
    return pl.BlockSpec(memory_space=pltpu.SMEM)


def anywhere():
    return pl.BlockSpec(memory_space=pl.ANY)


def call(body, outs, ins, specs, scratch=(), flops=1, name=None, out_specs=None, vmem=40):
    size = sum(math.prod(o) for o in outs) * 4 + sum(math.prod(x.shape) for x in ins) * 4
    return pl.pallas_call(
        body,
        out_shape=[jax.ShapeDtypeStruct(o, F32) for o in outs],
        grid=(1,),
        in_specs=specs,
        out_specs=out_specs or [whole(o) for o in outs],
        scratch_shapes=list(scratch),
        cost_estimate=pl.CostEstimate(flops=flops, bytes_accessed=size, transcendentals=0),
        compiler_params=pltpu.CompilerParams(vmem_limit_bytes=vmem * 1024 * 1024),
        name=name,
    )(*ins)


def ring_fields(axis, sign, ring, p, node, later):
    density, momenta = moments(p)
    wall = node == 2.0
    go, come = sided(axis, sign, ring)
    fields = [node, density, *momenta]
    fields += [jnp.where(wall, p[OPPOSITE[i]], p[i]) for i in go]
    return fields + [later(i) for i in come]


def first_x_body(fwd, later, des, node, up_out, down_out):
    for out, sign, planes, deep in (
        (up_out, 1, (BX - 1, BX - 2), slice(BX - DEEP, BX)),
        (down_out, -1, (0, 1), slice(0, DEEP)),
    ):
        out[DESIGN:] = des[deep]
        for ring, x in enumerate(planes):
            for h in (0, 8):
                rows = slice(h, h + 8)
                fields = ring_fields(
                    0,
                    sign,
                    ring,
                    [fwd[i, x, rows, :] for i in range(Q)],
                    node[x, rows, :].astype(F32),
                    lambda i, x=x, rows=rows: later[i, x, rows, :],
                )
                for k, value in enumerate(fields):
                    out[BASES[ring] + k, rows, :] = value


def first_x(fwd, later, design, node):
    ins = (fwd, later, design, node)
    return call(
        first_x_body, [(MSG, BY, NZ)] * 2, ins, [whole(x.shape) for x in ins], flops=800000, name="first_x"
    )


CHUNKS = ((0, 5), (5, 10), (10, 15), (15, 19))


def first_y_body(odd, fwd_any, later_any, design, node, near_out, far_out, fwd, later, up_out, down_out, sems):
    copies = [
        pltpu.make_async_copy(source.at[lo:hi], target.at[lo:hi], sems.at[k, c])
        for c, (lo, hi) in enumerate(CHUNKS)
        for k, (source, target) in enumerate(((fwd_any, fwd), (later_any, later)))
    ]
    for copy in copies:
        copy.start()
    for copy in copies:
        copy.wait()
    for out, sign, lines, deep in (
        (up_out, 1, (BY - 1, BY - 2), range(BY - DEEP, BY)),
        (down_out, -1, (0, 1), range(DEEP)),
    ):
        for k, y in enumerate(deep):
            out[DESIGN + k] = design[:, y, :]
        for ring, y in enumerate(lines):
            fields = ring_fields(
                1,
                sign,
                ring,
                [fwd[i, :, y, :] for i in range(Q)],
                node[:, y, :].astype(F32),
                lambda i, y=y: later[i, :, y, :],
            )
            for k, value in enumerate(fields):
                out[BASES[ring] + k] = value
    by_parity(odd, up_out, down_out, near_out, far_out)


def first_y(odd, fwd, later, design, node):
    block = pltpu.VMEM(fwd.shape, F32)
    return call(
        first_y_body,
        [(MSG, BX, NZ)] * 2,
        (odd, fwd, later, design, node),
        [scalar(), anywhere(), anywhere(), whole(design.shape), whole(node.shape)],
        scratch=(
            block,
            block,
            pltpu.VMEM((MSG, BX, NZ), F32),
            pltpu.VMEM((MSG, BX, NZ), F32),
            pltpu.SemaphoreType.DMA((2, len(CHUNKS))),
        ),
        flops=800000,
        name="first_y",
        vmem=60,
    )


def by_parity(odd, up, down, near_out, far_out):
    @pl.when(odd[0] == 0)
    def _():
        near_out[...] = up[...]
        far_out[...] = down[...]

    @pl.when(odd[0] == 1)
    def _():
        near_out[...] = down[...]
        far_out[...] = up[...]


def to_sides(odd, near, far, low, high):
    @pl.when(odd[0] == 0)
    def _():
        high[...] = near[...]
        low[...] = far[...]

    @pl.when(odd[0] == 1)
    def _():
        low[...] = near[...]
        high[...] = far[...]


def join_x_body(odd, own_up, own_down, near, far, up_out, down_out, low, high):
    to_sides(odd, near, far, low, high)
    for out, own, sign, planes, deep in (
        (up_out, own_up, 1, (BX - 1, BX - 2), range(BX - DEEP, BX)),
        (down_out, own_down, -1, (0, 1), range(DEEP)),
    ):
        out[...] = jnp.zeros_like(out)
        for k, x in enumerate(deep):
            base = design_row(k)
            out[base + DEEP : base + DEEP + BY, :] = own[DESIGN + k]
            for t in range(DEEP):
                out[base + t : base + t + 1, :] = low[DESIGN + t, x : x + 1, :]
                at = base + DEEP + BY + t
                out[at : at + 1, :] = high[DESIGN + t, x : x + 1, :]
        for ring, x in enumerate(planes):
            go, come = sided(0, sign, ring)
            fields = [(f, None) for f in range(MOVING)] + [("go", i) for i in go] + [("come", i) for i in come]
            for k, (field, i) in enumerate(fields):
                base = (BASES[ring] + k) * LINE
                out[base + 2 : base + 2 + BY, :] = own[BASES[ring] + k]
                for source, side, places in ((low, 1, (1, 0)), (high, -1, (2 + BY, 3 + BY))):
                    for other in (0, 1):
                        found = slot(1, side, other, field, i)
                        if found is not None:
                            at = base + places[other]
                            out[at : at + 1, :] = source[found, x : x + 1, :]


def join_x(odd, own_up, own_down, near, far):
    ins = (odd, own_up, own_down, near, far)
    return call(
        join_x_body,
        [(FLAT, NZ)] * 2,
        ins,
        [scalar()] + [whole(x.shape) for x in ins[1:]],
        scratch=(pltpu.VMEM((MSG, BX, NZ), F32),) * 2,
        flops=80000,
        name="join_x",
    )


EX = BX + 4
ROW = 8
PADY = 32


def main_body(
    odd, fwd, later_any, design, node, region, xlow, xhigh, near, far,
    adjoint_any, raw, part, up_out, down_out,
    ylow, yhigh, wide, kinds, fine, post, later, mid, flow, flux, first, adjoint, sem, sems,
):
    copy = pltpu.make_async_copy(later_any, later.at[:, 2 : 2 + BX, ROW : ROW + BY, :], sem)
    copy.start()
    to_sides(odd, near, far, ylow, yhigh)
    wide[...] = jnp.zeros_like(wide)
    wide[DEEP : DEEP + BX, ROW : ROW + BY, :] = design[...]
    for j in range(DEEP):
        at = design_row(j)
        wide[j, ROW - DEEP : ROW + BY + DEEP, :] = xlow[at : at + WIDE_LINE, :]
        wide[DEEP + BX + j, ROW - DEEP : ROW + BY + DEEP, :] = xhigh[at : at + WIDE_LINE, :]
        for x in range(BX):
            wide[DEEP + x, ROW - DEEP + j : ROW - DEEP + j + 1, :] = ylow[DESIGN + j, x : x + 1, :]
            wide[DEEP + x, ROW + BY + j : ROW + BY + j + 1, :] = yhigh[DESIGN + j, x : x + 1, :]
    long = slice(ROW - 2, ROW + BY + 2)
    xrings = ((1, xlow, 1, 0), (0, xlow, 1, 1), (2 + BX, xhigh, -1, 0), (3 + BX, xhigh, -1, 1))
    yrings = ((ROW - 1, ylow, 1, 0), (ROW - 2, ylow, 1, 1), (ROW + BY, yhigh, -1, 0), (ROW + BY + 1, yhigh, -1, 1))
    kinds[...] = jnp.zeros_like(kinds)
    kinds[2 : 2 + BX, ROW : ROW + BY, :] = node[...].astype(F32)

    def line(message, k):
        return message[k * LINE : (k + 1) * LINE, :]

    for x, message, sign, ring in xrings:
        kinds[x, long, :] = line(message, slot(0, sign, ring, KIND))
    for row, message, sign, ring in yrings:
        for x in range(BX):
            kinds[2 + x, row : row + 1, :] = message[slot(1, sign, ring, KIND), x : x + 1, :]
    inverse_norm = 1.0 / norm_row((8, NZ))

    def filter_plane(x, carry):
        for r in (4, 12, 20):
            value = filter_rows(lambda a, b: wide[x + RAD + a, r + b : r + b + 8, :]) * inverse_norm
            fine[x, r : r + 8, :] = value
        return carry

    lax.fori_loop(0, EX, filter_plane, 0)

    def factor_of(kind, filtered):
        return jnp.where(kind == 1.0, 1.0 - BRINKMAN * (1.0 - filtered), 1.0)

    for x, message, sign, ring in xrings:
        comps = sided(0, sign, ring)[0]
        kind = kinds[x, long, :]
        q = {i: line(message, slot(0, sign, ring, "go", i)) for i in comps}
        base = slot(0, sign, ring, DENS)
        value = post_tiles(
            comps, q, q, line(message, base), [line(message, base + 1 + a) for a in range(3)],
            kind, factor_of(kind, fine[x, long, :]),
        )
        for i in comps:
            post[i, x, long, :] = value[i]
    for row, message, sign, ring in yrings:
        comps = sided(1, sign, ring)[0]
        kind = kinds[2 : 2 + BX, row, :]
        q = {i: message[slot(1, sign, ring, "go", i)] for i in comps}
        base = slot(1, sign, ring, DENS)
        value = post_tiles(
            comps, q, q, message[base], [message[base + 1 + a] for a in range(3)],
            kind, factor_of(kind, fine[2 : 2 + BX, row, :]),
        )
        for i in comps:
            for x in range(BX):
                post[i, 2 + x, row : row + 1, :] = value[i][x : x + 1, :]

    def post_plane(x, carry):
        carry = list(carry)
        for h in (0, 8):
            rows = slice(h, h + 8)
            padded = slice(ROW + h, ROW + h + 8)
            p = [fwd[i, x, rows, :] for i in range(Q)]
            density, momenta = moments(p)
            kind = kinds[x + 2, padded, :]
            filtered = fine[x + 2, padded, :]
            inverse = 1.0 / density
            flow[0, x, rows, :] = density
            for a in range(3):
                flow[1 + a, x, rows, :] = momenta[a] * inverse
            bounced = [p[OPPOSITE[i]] for i in range(Q)]
            value = post_tiles(range(Q), p, bounced, density, momenta, kind, factor_of(kind, filtered))
            for i in range(Q):
                post[i, x + 2, padded, :] = value[i]
            counted = jnp.where(kind == 1.0, filtered, 0.0)
            where_region = region[x, rows, :]
            for r in range(REG):
                carry[r] = carry[r] + jnp.where(where_region == r, counted, 0.0)
        return tuple(carry)

    empty = jnp.zeros((8, NZ), F32)
    totals = lax.fori_loop(0, BX, post_plane, (empty,) * REG)
    copy.wait()
    for x, message, sign, ring in xrings:
        for i in sided(0, sign, ring)[1]:
            later[i, x, long, :] = line(message, slot(0, sign, ring, "come", i))
    for row, message, sign, ring in yrings:
        for i in sided(1, sign, ring)[1]:
            found = slot(1, sign, ring, "come", i)
            for x in range(BX):
                later[i, 2 + x, row : row + 1, :] = message[found, x : x + 1, :]

    def mid_plane(x, carry):
        for start in (ROW - 1, ROW + 7, ROW + 15):
            rows = slice(start, start + 8)
            density, mx, my, mz = 0.0, 0.0, 0.0, 0.0
            for cz in (0, 1, -1):
                p = {}
                for i in range(Q):
                    if VELOCITY[i][2] == cz:
                        at = start - VELOCITY[i][1]
                        p[i] = post[i, x + 1 - VELOCITY[i][0], at : at + 8, :]
                whole_sum = shift_z(add_all(p.values()), -cz)
                density = density + whole_sum
                if cz:
                    mz = mz + cz * whole_sum
                sides = []
                for a in range(2):
                    up = add_all(p[i] for i in p if VELOCITY[i][a] == 1)
                    down = add_all(p[i] for i in p if VELOCITY[i][a] == -1)
                    sides.append(shift_z(up - down, -cz))
                mx = mx + sides[0]
                my = my + sides[1]
            kind = kinds[x + 1, rows, :]
            outlet = kind == 4.0
            flux[x, rows, :] = jnp.where(outlet, mx, 0.0)
            inverse = 1.0 / density
            m = []
            for i in range(Q):
                at = start + VELOCITY[i][1]
                m.append(shift_z(later[i, x + 1 + VELOCITY[i][0], at : at + 8, :], VELOCITY[i][2]))
            value, gradient = back_tiles(
                m, density, [mx * inverse, my * inverse, mz * inverse], kind,
                factor_of(kind, fine[x + 1, rows, :]),
            )
            source = jnp.where(outlet, 1.0, 0.0)
            for i in range(Q):
                c = VELOCITY[i][0]
                mid[i, x, rows, :] = value[i] + c * source if c else value[i]
            first[x, rows, :] = gradient
        return carry

    lax.fori_loop(0, BX + 2, mid_plane, 0)
    raw_scale = BRINKMAN * inverse_norm

    def send(x):
        at = pl.ds(x, 1)
        return pltpu.make_async_copy(adjoint.at[:, at], adjoint_any.at[:, at], sems.at[x])

    def last_plane(x, carry):
        for h in (0, 8):
            rows = slice(h, h + 8)
            padded = slice(ROW + h, ROW + h + 8)
            kind = kinds[x + 2, padded, :]
            carry = carry + flux[x + 1, padded, :]
            m = []
            for i in range(Q):
                at = ROW + h + VELOCITY[i][1]
                m.append(shift_z(mid[i, x + 1 + VELOCITY[i][0], at : at + 8, :], VELOCITY[i][2]))
            value, gradient = back_tiles(
                m, flow[0, x, rows, :], [flow[1 + a, x, rows, :] for a in range(3)], kind,
                factor_of(kind, fine[x + 2, padded, :]),
            )
            for i in range(Q):
                adjoint[i, x, rows, :] = value[i]
            both = (first[x + 1, padded, :] + gradient) * raw_scale
            raw[x, rows, :] = jnp.where(kind == 1.0, both, 0.0)
        send(x).start()
        return carry

    totals = (*totals, lax.fori_loop(0, BX, last_plane, empty))
    row = jnp.zeros((8, NZ), F32)
    for r, value in enumerate(totals):
        row = jnp.where(lanes((8, NZ)) == r, jnp.sum(value, axis=(0, 1), keepdims=True), row)
    part[...] = row
    for out, begin in ((up_out, BX - RAD), (down_out, 0)):
        for j in range(RAD):
            out[j * BY : (j + 1) * BY, :] = raw[begin + j]
        out[RAW_ROWS:, :] = row
    for x in range(BX):
        send(x).wait()


def main(odd, fwd, later, design, node, region, xlow, xhigh, near, far):
    ins = (odd, fwd, later, design, node, region, xlow, xhigh, near, far)
    specs = [scalar()] + [whole(x.shape) for x in ins[1:]]
    specs[2] = anywhere()
    outs = [(Q, BX, BY, NZ), (BX, BY, NZ), (8, NZ), (RAW_ROWS + 8, NZ), (RAW_ROWS + 8, NZ)]
    return call(
        main_body,
        outs,
        ins,
        specs,
        scratch=(
            pltpu.VMEM((MSG, BX, NZ), F32),
            pltpu.VMEM((MSG, BX, NZ), F32),
            pltpu.VMEM((BX + 2 * DEEP, PADY, NZ), F32),
            pltpu.VMEM((EX, PADY, NZ), F32),
            pltpu.VMEM((EX, PADY, NZ), F32),
            pltpu.VMEM((Q, EX, PADY, NZ), F32),
            pltpu.VMEM((Q, EX, PADY, NZ), F32),
            pltpu.VMEM((Q, BX + 2, PADY, NZ), F32),
            pltpu.VMEM((4, BX, BY, NZ), F32),
            pltpu.VMEM((BX + 2, PADY, NZ), F32),
            pltpu.VMEM((BX + 2, PADY, NZ), F32),
            pltpu.VMEM((Q, BX, BY, NZ), F32),
            pltpu.SemaphoreType.DMA,
            pltpu.SemaphoreType.DMA((BX,)),
        ),
        flops=30000000,
        name="main",
        out_specs=[anywhere()] + [whole(o) for o in outs[1:]],
    )


def raw_y_body(odd, raw, part, low, high, near_out, far_out, rows_out, up_out, down_out):
    for out, begin in ((up_out, BY - RAD), (down_out, 0)):
        out[...] = jnp.zeros_like(out)
        for j in range(RAD):
            y = begin + j
            out[j, RAD : RAD + BX, :] = raw[:, y, :]
            for x in range(RAD):
                out[j, x : x + 1, :] = low[x * BY + y : x * BY + y + 1, :]
                out[j, RAD + BX + x : RAD + BX + x + 1, :] = high[x * BY + y : x * BY + y + 1, :]
    by_parity(odd, up_out, down_out, near_out, far_out)
    other = jnp.where(odd[1] == 1, low[RAW_ROWS : RAW_ROWS + 8, :], high[RAW_ROWS : RAW_ROWS + 8, :])
    row = part[...] + other
    for k in range(0, rows_out.shape[0], 8):
        rows_out[k : k + 8, :] = row


def raw_y(odd, raw, part, low, high, count):
    ins = (odd, raw, part, low, high)
    return call(
        raw_y_body,
        [(RAD, BY, NZ), (RAD, BY, NZ), (count, NZ)],
        ins,
        [scalar()] + [whole(x.shape) for x in ins[1:]],
        scratch=(pltpu.VMEM((RAD, BY, NZ), F32),) * 2,
        flops=20000,
        name="raw_y",
    )


def spread_body(odd, raw, xlow, xhigh, near, far, rows, out, objective, volumes, ylow, yhigh, wide):
    to_sides(odd, near, far, ylow, yhigh)
    wide[RAD : RAD + BX, ROW : ROW + BY, :] = raw[...]
    for j in range(RAD):
        wide[j, ROW : ROW + BY, :] = xlow[j * BY : (j + 1) * BY, :]
        wide[RAD + BX + j, ROW : ROW + BY, :] = xhigh[j * BY : (j + 1) * BY, :]
    for x in range(BX + 2 * RAD):
        for j in range(RAD):
            wide[x, ROW - RAD + j : ROW - RAD + j + 1, :] = ylow[j, x : x + 1, :]
            wide[x, ROW + BY + j : ROW + BY + j + 1, :] = yhigh[j, x : x + 1, :]

    def plane(x, carry):
        for h in (0, 8):
            at = ROW + h
            out[x, h : h + 8, :] = filter_rows(lambda a, b: wide[x + RAD + a, at + b : at + b + 8, :])
        return carry

    lax.fori_loop(0, BX, plane, 0)
    total = add_all(rows[k : k + 8, :] for k in range(0, rows.shape[0], 8))
    lane = lanes((8, NZ))
    for r in range(REG + 1):
        value = jnp.sum(jnp.where(lane == r, total, 0.0))
        if r < REG:
            volumes[r] = value
        else:
            objective[0] = value


def spread(odd, raw, xlow, xhigh, near, far, rows):
    ins = (odd, raw, xlow, xhigh, near, far, rows)
    return call(
        spread_body,
        [(BX, BY, NZ), (1,), (REG,)],
        ins,
        [scalar()] + [whole(x.shape) for x in ins[1:]],
        scratch=(pltpu.VMEM((RAD, BY, NZ), F32),) * 2 + (pltpu.VMEM((BX + 2 * RAD, PADY, NZ), F32),),
        flops=2000000,
        name="spread",
        out_specs=[whole((BX, BY, NZ)), scalar(), scalar()],
    )


def exchange(up, down, axis):
    count = lax.axis_size(axis)
    forward = [(i, (i + 1) % count) for i in range(count)]
    backward = [(j, i) for i, j in forward]
    return lax.ppermute(up, axis, forward), lax.ppermute(down, axis, backward)


def swap(near, far, axis):
    count = lax.axis_size(axis)
    inner = [(i, i ^ 1) for i in range(count)]
    outer = [(i, (i + 1 if i % 2 else i - 1) % count) for i in range(count)]
    return lax.ppermute(near, axis, inner), lax.ppermute(far, axis, outer)


def share(rows):
    nx, ny = lax.axis_size("gx"), lax.axis_size("gy")
    groups = [[x * ny + y for x in range(p, nx, 2) for y in range(ny)] for p in (0, 1)]
    return lax.all_to_all(rows, ("gx", "gy"), 0, 0, tiled=True, axis_index_groups=groups)


def per_device(forward_pops, later_adjoint, design, node_type, region):
    odd = jnp.stack([lax.axis_index("gy") % 2, lax.axis_index("gx") % 2]).astype(jnp.int32)
    near, far = swap(*first_y(odd, forward_pops, later_adjoint, design, node_type), "gy")
    own_up, own_down = first_x(forward_pops, later_adjoint, design, node_type)
    xlow, xhigh = exchange(*join_x(odd, own_up, own_down, near, far), "gx")
    adjoint, raw, part, up, down = main(
        odd, forward_pops, later_adjoint, design, node_type, region, xlow, xhigh, near, far
    )
    xlow, xhigh = exchange(up, down, "gx")
    pairs = lax.axis_size("gx") * lax.axis_size("gy") // 2
    near, far, rows = raw_y(odd, raw, part, xlow, xhigh, pairs)
    rows = share(rows)
    near, far = swap(near, far, "gy")
    sensitivity, objective, volumes = spread(odd, raw, xlow, xhigh, near, far, rows)
    return adjoint, sensitivity, objective[0], volumes


def solution(mesh):
    cells = P("gx", "gy", None)
    pops = P(None, "gx", "gy", None)
    return jax.shard_map(
        per_device,
        mesh=mesh,
        in_specs=(pops, pops, cells, cells, cells),
        out_specs=(pops, cells, P(), P()),
        check_vma=False,
    )
```

```python
import math

import jax
import jax.numpy as jnp
from jax import lax
from jax.experimental import pallas as pl
from jax.experimental.pallas import tpu as pltpu
from jax.sharding import PartitionSpec as P

RAD = 3
REG = 8
VELOCITY = [
    (0, 0, 0),
    (1, 0, 0),
    (-1, 0, 0),
    (0, 1, 0),
    (0, -1, 0),
    (0, 0, 1),
    (0, 0, -1),
    (1, 1, 0),
    (-1, -1, 0),
    (1, -1, 0),
    (-1, 1, 0),
    (1, 0, 1),
    (-1, 0, -1),
    (1, 0, -1),
    (-1, 0, 1),
    (0, 1, 1),
    (0, -1, -1),
    (0, 1, -1),
    (0, -1, 1),
]
WEIGHTS = [1.0 / 3.0] + [1.0 / 18.0] * 6 + [1.0 / 36.0] * 12
OPPOSITE = [0, 2, 1, 4, 3, 6, 5, 8, 7, 10, 9, 12, 11, 14, 13, 16, 15, 18, 17]
RELAXATION = 1.0 / 0.6
BRINKMAN = 0.9
Q = 19
BX = 8
BY = 16
NZ = 128
F32 = jnp.float32


KIND, DENS, MOVING = 0, 1, 5
DEEP = RAD + 2


def sided(axis, sign, ring):
    keep = (lambda c: c >= 0) if ring == 0 else (lambda c: c > 0)
    go = [i for i in range(Q) if keep(sign * VELOCITY[i][axis])]
    come = [i for i in range(Q) if keep(-sign * VELOCITY[i][axis])]
    return go, come


SIZES = [MOVING + sum(map(len, sided(0, 1, ring))) for ring in (0, 1)]
BASES = (0, SIZES[0])
DESIGN = sum(SIZES)
MSG = DESIGN + DEEP
LINE = BY + 4
WIDE_LINE = BY + 2 * DEEP
FLAT = (DESIGN * LINE + DEEP * WIDE_LINE + 7) // 8 * 8
RAW_ROWS = RAD * BY


def design_row(j):
    return DESIGN * LINE + j * WIDE_LINE


def slot(axis, sign, ring, field, which=None):
    base = BASES[ring]
    if field in ("go", "come"):
        go, come = sided(axis, sign, ring)
        listed = go if field == "go" else come
        if which not in listed:
            return None
        return base + MOVING + (0 if field == "go" else len(go)) + listed.index(which)
    return base + field


CLASSES = sorted(
    {a * a + b * b for a in range(RAD + 1) for b in range(RAD + 1) if a * a + b * b < (RAD + 1) ** 2}
)
TAPS = {
    s: [
        (a, b)
        for a in range(-RAD, RAD + 1)
        for b in range(-RAD, RAD + 1)
        if a * a + b * b == s
    ]
    for s in CLASSES
}


def tap_weight(s, c):
    return RAD + 1 - math.sqrt(s + c * c)


def lanes(shape):
    return lax.broadcasted_iota(jnp.int32, shape, len(shape) - 1)


def shift_z(value, c):
    if c == 0:
        return value
    z = lanes(value.shape)
    moved = pltpu.roll(value, (-c) % NZ, value.ndim - 1)
    return jnp.where((z + c >= 0) & (z + c < NZ), moved, 0.0)


def norm_row(shape):
    z = lanes(shape)
    result = None
    for c in range(RAD + 1):
        total = sum(len(TAPS[s]) * tap_weight(s, c) for s in CLASSES if tap_weight(s, c) > 0)
        if c == 0:
            result = jnp.full(shape, total, F32)
        else:
            result = result + jnp.where(z >= c, total, 0.0) + jnp.where(z < NZ - c, total, 0.0)
    return result


def filter_rows(load):
    sums = []
    for s in CLASSES:
        running = None
        for a, b in TAPS[s]:
            tile = load(a, b)
            running = tile if running is None else running + tile
        sums.append(running)
    result = None
    for c in range(RAD + 1):
        mixed = None
        for s, part in zip(CLASSES, sums):
            if tap_weight(s, c) > 0:
                term = tap_weight(s, c) * part
                mixed = term if mixed is None else mixed + term
        if c == 0:
            result = mixed
        else:
            result = result + shift_z(mixed, c) + shift_z(mixed, -c)
    return result


def add_all(values):
    values = list(values)
    while len(values) > 1:
        values = [
            values[k] + values[k + 1] if k + 1 < len(values) else values[k]
            for k in range(0, len(values), 2)
        ]
    return values[0]


def moments(p):
    momenta = []
    for a in range(3):
        up = add_all(p[i] for i in range(Q) if VELOCITY[i][a] == 1)
        down = add_all(p[i] for i in range(Q) if VELOCITY[i][a] == -1)
        momenta.append(up - down)
    return add_all(p), momenta


def along(i, vector):
    result = None
    for a in range(3):
        c = VELOCITY[i][a]
        if c == 0:
            continue
        if result is None:
            result = vector[a] if c == 1 else -vector[a]
        else:
            result = result + vector[a] if c == 1 else result - vector[a]
    return result


def post_tiles(which, straight, bounced, density, momenta, node, factor):
    inverse = 1.0 / density
    u = [factor * (m * inverse) for m in momenta]
    rest = 1.0 - 1.5 * (u[0] * u[0] + u[1] * u[1] + u[2] * u[2])
    rate = jnp.where(node <= 1.5, RELAXATION, 1.0)
    keep = 1.0 - rate
    wall = node == 2.0
    scale = rate * density
    result = {}
    for i in which:
        a = along(i, u)
        form = rest if a is None else rest + a * (3.0 + 4.5 * a)
        relaxed = keep * straight[i] + (WEIGHTS[i] * scale) * form
        result[i] = jnp.where(wall, bounced[i], relaxed)
    return result


def back_tiles(m, density, plain, node, factor):
    u = [factor * q for q in plain]
    rate = jnp.where(node <= 1.5, RELAXATION, 1.0)
    keep = 1.0 - rate
    wall = node == 2.0

    def weighted(select):
        total = None
        for w, group in ((1.0 / 18.0, range(1, 7)), (1.0 / 36.0, range(7, Q))):
            up = [m[i] for i in group if select(VELOCITY[i]) > 0]
            down = [m[i] for i in group if select(VELOCITY[i]) < 0]
            if not up and not down:
                continue
            value = add_all(up)
            if down:
                value = value - add_all(down)
            value = w * value
            total = value if total is None else total + value
        return total

    zero = (1.0 / 3.0) * m[0] + weighted(lambda c: 1)
    one = [weighted(lambda c, a=a: c[a]) for a in range(3)]
    two = {}
    for a in range(3):
        for b in range(a, 3):
            two[a, b] = two[b, a] = weighted(lambda c, a=a, b=b: c[a] * c[b])
    bent = [two[a, 0] * u[0] + two[a, 1] * u[1] + two[a, 2] * u[2] for a in range(3)]
    dot = lambda p, q: p[0] * q[0] + p[1] * q[1] + p[2] * q[2]
    scalar = zero * (1.0 - 1.5 * dot(u, u)) + 3.0 * dot(one, u) + 4.5 * dot(bent, u)
    vector = [3.0 * (one[a] + 3.0 * bent[a] - zero * u[a]) for a in range(3)]
    start = rate * (scalar - dot(vector, u))
    slope = [(rate * factor) * v for v in vector]
    result = []
    for i in range(Q):
        lean = along(i, slope)
        relaxed = keep * m[i] + (start if lean is None else start + lean)
        result.append(jnp.where(wall, m[OPPOSITE[i]], relaxed))
    gradient = jnp.where(wall, 0.0, rate * density * dot(vector, plain))
    return result, gradient


def whole(shape):
    return pl.BlockSpec(shape, lambda *_: (0,) * len(shape))


def scalar():
    return pl.BlockSpec(memory_space=pltpu.SMEM)


def anywhere():
    return pl.BlockSpec(memory_space=pl.ANY)


def call(body, outs, ins, specs, scratch=(), flops=1, name=None, out_specs=None, vmem=40):
    size = sum(math.prod(o) for o in outs) * 4 + sum(math.prod(x.shape) for x in ins) * 4
    return pl.pallas_call(
        body,
        out_shape=[jax.ShapeDtypeStruct(o, F32) for o in outs],
        grid=(1,),
        in_specs=specs,
        out_specs=out_specs or [whole(o) for o in outs],
        scratch_shapes=list(scratch),
        cost_estimate=pl.CostEstimate(flops=flops, bytes_accessed=size, transcendentals=0),
        compiler_params=pltpu.CompilerParams(vmem_limit_bytes=vmem * 1024 * 1024),
        name=name,
    )(*ins)


def ring_fields(axis, sign, ring, p, node, later):
    density, momenta = moments(p)
    wall = node == 2.0
    go, come = sided(axis, sign, ring)
    fields = [node, density, *momenta]
    fields += [jnp.where(wall, p[OPPOSITE[i]], p[i]) for i in go]
    return fields + [later(i) for i in come]


def first_x_body(fwd, later, des, node, up_out, down_out):
    for out, sign, planes, deep in (
        (up_out, 1, (BX - 1, BX - 2), slice(BX - DEEP, BX)),
        (down_out, -1, (0, 1), slice(0, DEEP)),
    ):
        out[DESIGN:] = des[deep]
        for ring, x in enumerate(planes):
            for h in (0, 8):
                rows = slice(h, h + 8)
                fields = ring_fields(
                    0,
                    sign,
                    ring,
                    [fwd[i, x, rows, :] for i in range(Q)],
                    node[x, rows, :].astype(F32),
                    lambda i, x=x, rows=rows: later[i, x, rows, :],
                )
                for k, value in enumerate(fields):
                    out[BASES[ring] + k, rows, :] = value


def first_x(fwd, later, design, node):
    ins = (fwd, later, design, node)
    return call(
        first_x_body, [(MSG, BY, NZ)] * 2, ins, [whole(x.shape) for x in ins], flops=800000, name="first_x"
    )


def first_y_body(fwd_any, later_any, design, node, far_out, near_out, fwd, later, up_out, down_out, sems):
    copies = [
        pltpu.make_async_copy(source.at[:, :, at : at + 2, :], target.at[:, :, to : to + 2, :], sems.at[k, e])
        for e, (at, to) in enumerate(((0, 0), (BY - 2, 2)))
        for k, (source, target) in enumerate(((fwd_any, fwd), (later_any, later)))
    ]
    for copy in copies:
        copy.start()
    for copy in copies:
        copy.wait()
    for out, sign, lines, deep in (
        (up_out, 1, (BY - 1, BY - 2), range(BY - DEEP, BY)),
        (down_out, -1, (0, 1), range(DEEP)),
    ):
        for k, y in enumerate(deep):
            out[DESIGN + k] = design[:, y, :]
        for ring, y in enumerate(lines):
            fields = ring_fields(
                1,
                sign,
                ring,
                [fwd[i, :, y % 12, :] for i in range(Q)],
                node[:, y, :].astype(F32),
                lambda i, y=y: later[i, :, y % 12, :],
            )
            for k, value in enumerate(fields):
                out[BASES[ring] + k] = value
    by_parity("gy", up_out, down_out, far_out, near_out)


def first_y(fwd, later, design, node):
    block = pltpu.VMEM((Q, BX, 4, NZ), F32)
    return call(
        first_y_body,
        [(MSG, BX, NZ)] * 2,
        (fwd, later, design, node),
        [anywhere(), anywhere(), whole(design.shape), whole(node.shape)],
        scratch=(
            block,
            block,
            pltpu.VMEM((MSG, BX, NZ), F32),
            pltpu.VMEM((MSG, BX, NZ), F32),
            pltpu.SemaphoreType.DMA((2, 2)),
        ),
        flops=800000,
        name="first_y",
        vmem=60,
    )


def odd(axis):
    return lax.rem(lax.axis_index(axis), 2)


def by_parity(axis, up, down, far_out, near_out):
    @pl.when(odd(axis) == 0)
    def _():
        near_out[...] = up[...]
        far_out[...] = down[...]

    @pl.when(odd(axis) == 1)
    def _():
        near_out[...] = down[...]
        far_out[...] = up[...]


def to_sides(axis, far, near, low, high):
    @pl.when(odd(axis) == 0)
    def _():
        high[...] = near[...]
        low[...] = far[...]

    @pl.when(odd(axis) == 1)
    def _():
        low[...] = near[...]
        high[...] = far[...]


def join_x_body(own_up, own_down, far, near, up_out, down_out, low, high):
    to_sides("gy", far, near, low, high)
    for out, own, sign, planes, deep in (
        (up_out, own_up, 1, (BX - 1, BX - 2), range(BX - DEEP, BX)),
        (down_out, own_down, -1, (0, 1), range(DEEP)),
    ):
        out[...] = jnp.zeros_like(out)
        for k, x in enumerate(deep):
            base = design_row(k)
            out[base + DEEP : base + DEEP + BY, :] = own[DESIGN + k]
            for t in range(DEEP):
                out[base + t : base + t + 1, :] = low[DESIGN + t, x : x + 1, :]
                at = base + DEEP + BY + t
                out[at : at + 1, :] = high[DESIGN + t, x : x + 1, :]
        for ring, x in enumerate(planes):
            go, come = sided(0, sign, ring)
            fields = [(f, None) for f in range(MOVING)] + [("go", i) for i in go] + [("come", i) for i in come]
            for k, (field, i) in enumerate(fields):
                base = (BASES[ring] + k) * LINE
                out[base + 2 : base + 2 + BY, :] = own[BASES[ring] + k]
                for source, side, places in ((low, 1, (1, 0)), (high, -1, (2 + BY, 3 + BY))):
                    for other in (0, 1):
                        found = slot(1, side, other, field, i)
                        if found is not None:
                            at = base + places[other]
                            out[at : at + 1, :] = source[found, x : x + 1, :]


def join_x(own_up, own_down, far, near):
    ins = (own_up, own_down, far, near)
    return call(
        join_x_body,
        [(FLAT, NZ)] * 2,
        ins,
        [whole(x.shape) for x in ins],
        scratch=(pltpu.VMEM((MSG, BX, NZ), F32),) * 2,
        flops=80000,
        name="join_x",
    )


EX = BX + 4
ROW = 8
PADY = 32


def main_body(
    fwd, later_any, design, node, region, xlow, xhigh, far, near,
    adjoint_any, raw, part, up_out, down_out,
    ylow, yhigh, wide, kinds, fine, post, later, mid, flow, flux, first, adjoint, sem, sems,
):
    copy = pltpu.make_async_copy(later_any, later.at[:, 2 : 2 + BX, ROW : ROW + BY, :], sem)
    copy.start()
    to_sides("gy", far, near, ylow, yhigh)
    wide[...] = jnp.zeros_like(wide)
    wide[DEEP : DEEP + BX, ROW : ROW + BY, :] = design[...]
    for j in range(DEEP):
        at = design_row(j)
        wide[j, ROW - DEEP : ROW + BY + DEEP, :] = xlow[at : at + WIDE_LINE, :]
        wide[DEEP + BX + j, ROW - DEEP : ROW + BY + DEEP, :] = xhigh[at : at + WIDE_LINE, :]
        for x in range(BX):
            wide[DEEP + x, ROW - DEEP + j : ROW - DEEP + j + 1, :] = ylow[DESIGN + j, x : x + 1, :]
            wide[DEEP + x, ROW + BY + j : ROW + BY + j + 1, :] = yhigh[DESIGN + j, x : x + 1, :]
    long = slice(ROW - 2, ROW + BY + 2)
    xrings = ((1, xlow, 1, 0), (0, xlow, 1, 1), (2 + BX, xhigh, -1, 0), (3 + BX, xhigh, -1, 1))
    yrings = ((ROW - 1, ylow, 1, 0), (ROW - 2, ylow, 1, 1), (ROW + BY, yhigh, -1, 0), (ROW + BY + 1, yhigh, -1, 1))
    kinds[...] = jnp.zeros_like(kinds)
    kinds[2 : 2 + BX, ROW : ROW + BY, :] = node[...].astype(F32)

    def line(message, k):
        return message[k * LINE : (k + 1) * LINE, :]

    for x, message, sign, ring in xrings:
        kinds[x, long, :] = line(message, slot(0, sign, ring, KIND))
    for row, message, sign, ring in yrings:
        for x in range(BX):
            kinds[2 + x, row : row + 1, :] = message[slot(1, sign, ring, KIND), x : x + 1, :]
    inverse_norm = 1.0 / norm_row((8, NZ))

    def filter_plane(x, carry):
        for r in (4, 12, 20):
            value = filter_rows(lambda a, b: wide[x + RAD + a, r + b : r + b + 8, :]) * inverse_norm
            fine[x, r : r + 8, :] = value
        return carry

    lax.fori_loop(0, EX, filter_plane, 0)

    def factor_of(kind, filtered):
        return jnp.where(kind == 1.0, 1.0 - BRINKMAN * (1.0 - filtered), 1.0)

    for x, message, sign, ring in xrings:
        comps = sided(0, sign, ring)[0]
        kind = kinds[x, long, :]
        q = {i: line(message, slot(0, sign, ring, "go", i)) for i in comps}
        base = slot(0, sign, ring, DENS)
        value = post_tiles(
            comps, q, q, line(message, base), [line(message, base + 1 + a) for a in range(3)],
            kind, factor_of(kind, fine[x, long, :]),
        )
        for i in comps:
            post[i, x, long, :] = value[i]
    for row, message, sign, ring in yrings:
        comps = sided(1, sign, ring)[0]
        kind = kinds[2 : 2 + BX, row, :]
        q = {i: message[slot(1, sign, ring, "go", i)] for i in comps}
        base = slot(1, sign, ring, DENS)
        value = post_tiles(
            comps, q, q, message[base], [message[base + 1 + a] for a in range(3)],
            kind, factor_of(kind, fine[2 : 2 + BX, row, :]),
        )
        for i in comps:
            for x in range(BX):
                post[i, 2 + x, row : row + 1, :] = value[i][x : x + 1, :]

    def post_plane(x, carry):
        carry = list(carry)
        for h in (0, 8):
            rows = slice(h, h + 8)
            padded = slice(ROW + h, ROW + h + 8)
            p = [fwd[i, x, rows, :] for i in range(Q)]
            density, momenta = moments(p)
            kind = kinds[x + 2, padded, :]
            filtered = fine[x + 2, padded, :]
            inverse = 1.0 / density
            flow[0, x, rows, :] = density
            for a in range(3):
                flow[1 + a, x, rows, :] = momenta[a] * inverse
            bounced = [p[OPPOSITE[i]] for i in range(Q)]
            value = post_tiles(range(Q), p, bounced, density, momenta, kind, factor_of(kind, filtered))
            for i in range(Q):
                post[i, x + 2, padded, :] = value[i]
            counted = jnp.where(kind == 1.0, filtered, 0.0)
            where_region = region[x, rows, :]
            for r in range(REG):
                carry[r] = carry[r] + jnp.where(where_region == r, counted, 0.0)
        return tuple(carry)

    empty = jnp.zeros((8, NZ), F32)
    totals = lax.fori_loop(0, BX, post_plane, (empty,) * REG)
    copy.wait()
    for x, message, sign, ring in xrings:
        for i in sided(0, sign, ring)[1]:
            later[i, x, long, :] = line(message, slot(0, sign, ring, "come", i))
    for row, message, sign, ring in yrings:
        for i in sided(1, sign, ring)[1]:
            found = slot(1, sign, ring, "come", i)
            for x in range(BX):
                later[i, 2 + x, row : row + 1, :] = message[found, x : x + 1, :]

    def mid_plane(x, carry):
        for start in (ROW - 1, ROW + 7, ROW + 15):
            rows = slice(start, start + 8)
            density, mx, my, mz = 0.0, 0.0, 0.0, 0.0
            for cz in (0, 1, -1):
                p = {}
                for i in range(Q):
                    if VELOCITY[i][2] == cz:
                        at = start - VELOCITY[i][1]
                        p[i] = post[i, x + 1 - VELOCITY[i][0], at : at + 8, :]
                whole_sum = shift_z(add_all(p.values()), -cz)
                density = density + whole_sum
                if cz:
                    mz = mz + cz * whole_sum
                sides = []
                for a in range(2):
                    up = add_all(p[i] for i in p if VELOCITY[i][a] == 1)
                    down = add_all(p[i] for i in p if VELOCITY[i][a] == -1)
                    sides.append(shift_z(up - down, -cz))
                mx = mx + sides[0]
                my = my + sides[1]
            kind = kinds[x + 1, rows, :]
            outlet = kind == 4.0
            flux[x, rows, :] = jnp.where(outlet, mx, 0.0)
            inverse = 1.0 / density
            m = []
            for i in range(Q):
                at = start + VELOCITY[i][1]
                m.append(shift_z(later[i, x + 1 + VELOCITY[i][0], at : at + 8, :], VELOCITY[i][2]))
            value, gradient = back_tiles(
                m, density, [mx * inverse, my * inverse, mz * inverse], kind,
                factor_of(kind, fine[x + 1, rows, :]),
            )
            source = jnp.where(outlet, 1.0, 0.0)
            for i in range(Q):
                c = VELOCITY[i][0]
                mid[i, x, rows, :] = value[i] + c * source if c else value[i]
            first[x, rows, :] = gradient
        return carry

    lax.fori_loop(0, BX + 2, mid_plane, 0)
    raw_scale = BRINKMAN * inverse_norm

    def send(x):
        at = pl.ds(x, 1)
        return pltpu.make_async_copy(adjoint.at[:, at], adjoint_any.at[:, at], sems.at[x])

    def last_plane(x, carry):
        for h in (0, 8):
            rows = slice(h, h + 8)
            padded = slice(ROW + h, ROW + h + 8)
            kind = kinds[x + 2, padded, :]
            carry = carry + flux[x + 1, padded, :]
            m = []
            for i in range(Q):
                at = ROW + h + VELOCITY[i][1]
                m.append(shift_z(mid[i, x + 1 + VELOCITY[i][0], at : at + 8, :], VELOCITY[i][2]))
            value, gradient = back_tiles(
                m, flow[0, x, rows, :], [flow[1 + a, x, rows, :] for a in range(3)], kind,
                factor_of(kind, fine[x + 2, padded, :]),
            )
            for i in range(Q):
                adjoint[i, x, rows, :] = value[i]
            both = (first[x + 1, padded, :] + gradient) * raw_scale
            raw[x, rows, :] = jnp.where(kind == 1.0, both, 0.0)
        send(x).start()
        return carry

    totals = (*totals, lax.fori_loop(0, BX, last_plane, empty))
    row = jnp.zeros((8, NZ), F32)
    for r, value in enumerate(totals):
        row = jnp.where(lanes((8, NZ)) == r, jnp.sum(value, axis=(0, 1), keepdims=True), row)
    part[...] = row
    for out, begin in ((up_out, BX - RAD), (down_out, 0)):
        for j in range(RAD):
            out[j * BY : (j + 1) * BY, :] = raw[begin + j]
        out[RAW_ROWS:, :] = row
    for x in range(BX):
        send(x).wait()


def main(fwd, later, design, node, region, xlow, xhigh, far, near):
    ins = (fwd, later, design, node, region, xlow, xhigh, far, near)
    specs = [whole(x.shape) for x in ins]
    specs[1] = anywhere()
    outs = [(Q, BX, BY, NZ), (BX, BY, NZ), (8, NZ), (RAW_ROWS + 8, NZ), (RAW_ROWS + 8, NZ)]
    return call(
        main_body,
        outs,
        ins,
        specs,
        scratch=(
            pltpu.VMEM((MSG, BX, NZ), F32),
            pltpu.VMEM((MSG, BX, NZ), F32),
            pltpu.VMEM((BX + 2 * DEEP, PADY, NZ), F32),
            pltpu.VMEM((EX, PADY, NZ), F32),
            pltpu.VMEM((EX, PADY, NZ), F32),
            pltpu.VMEM((Q, EX, PADY, NZ), F32),
            pltpu.VMEM((Q, EX, PADY, NZ), F32),
            pltpu.VMEM((Q, BX + 2, PADY, NZ), F32),
            pltpu.VMEM((4, BX, BY, NZ), F32),
            pltpu.VMEM((BX + 2, PADY, NZ), F32),
            pltpu.VMEM((BX + 2, PADY, NZ), F32),
            pltpu.VMEM((Q, BX, BY, NZ), F32),
            pltpu.SemaphoreType.DMA,
            pltpu.SemaphoreType.DMA((BX,)),
        ),
        flops=30000000,
        name="main",
        out_specs=[anywhere()] + [whole(o) for o in outs[1:]],
    )


def raw_y_body(raw, part, low, high, far_out, near_out, rows_out, up_out, down_out):
    for out, begin in ((up_out, BY - RAD), (down_out, 0)):
        out[...] = jnp.zeros_like(out)
        for j in range(RAD):
            y = begin + j
            out[j, RAD : RAD + BX, :] = raw[:, y, :]
            for x in range(RAD):
                out[j, x : x + 1, :] = low[x * BY + y : x * BY + y + 1, :]
                out[j, RAD + BX + x : RAD + BX + x + 1, :] = high[x * BY + y : x * BY + y + 1, :]
    by_parity("gy", up_out, down_out, far_out, near_out)
    other = jnp.where(odd("gx") == 1, low[RAW_ROWS : RAW_ROWS + 8, :], high[RAW_ROWS : RAW_ROWS + 8, :])
    row = part[...] + other
    for k in range(0, rows_out.shape[0], 8):
        rows_out[k : k + 8, :] = row


def raw_y(raw, part, low, high, count):
    ins = (raw, part, low, high)
    return call(
        raw_y_body,
        [(RAD, BY, NZ), (RAD, BY, NZ), (count, NZ)],
        ins,
        [whole(x.shape) for x in ins],
        scratch=(pltpu.VMEM((RAD, BY, NZ), F32),) * 2,
        flops=20000,
        name="raw_y",
    )


def spread_body(raw, xlow, xhigh, far, near, rows, out, objective, volumes, ylow, yhigh, wide):
    to_sides("gy", far, near, ylow, yhigh)
    wide[RAD : RAD + BX, ROW : ROW + BY, :] = raw[...]
    for j in range(RAD):
        wide[j, ROW : ROW + BY, :] = xlow[j * BY : (j + 1) * BY, :]
        wide[RAD + BX + j, ROW : ROW + BY, :] = xhigh[j * BY : (j + 1) * BY, :]
    for x in range(BX + 2 * RAD):
        for j in range(RAD):
            wide[x, ROW - RAD + j : ROW - RAD + j + 1, :] = ylow[j, x : x + 1, :]
            wide[x, ROW + BY + j : ROW + BY + j + 1, :] = yhigh[j, x : x + 1, :]

    def plane(x, carry):
        for h in (0, 8):
            at = ROW + h
            out[x, h : h + 8, :] = filter_rows(lambda a, b: wide[x + RAD + a, at + b : at + b + 8, :])
        return carry

    lax.fori_loop(0, BX, plane, 0)
    total = add_all(rows[k : k + 8, :] for k in range(0, rows.shape[0], 8))
    lane = lanes((8, NZ))
    for r in range(REG + 1):
        value = jnp.sum(jnp.where(lane == r, total, 0.0))
        if r < REG:
            volumes[r] = value
        else:
            objective[0] = value


def spread(raw, xlow, xhigh, far, near, rows):
    ins = (raw, xlow, xhigh, far, near, rows)
    return call(
        spread_body,
        [(BX, BY, NZ), (1,), (REG,)],
        ins,
        [whole(x.shape) for x in ins],
        scratch=(pltpu.VMEM((RAD, BY, NZ), F32),) * 2 + (pltpu.VMEM((BX + 2 * RAD, PADY, NZ), F32),),
        flops=2000000,
        name="spread",
        out_specs=[whole((BX, BY, NZ)), scalar(), scalar()],
    )


def exchange(up, down, axis):
    count = lax.axis_size(axis)
    forward = [(i, (i + 1) % count) for i in range(count)]
    backward = [(j, i) for i, j in forward]
    return lax.ppermute(up, axis, forward), lax.ppermute(down, axis, backward)


def swap(far, near, axis):
    count = lax.axis_size(axis)
    inner = [(i, i ^ 1) for i in range(count)]
    outer = [(i, (i + 1 if i % 2 else i - 1) % count) for i in range(count)]
    return lax.ppermute(far, axis, outer), lax.ppermute(near, axis, inner)


def share(rows):
    nx, ny = lax.axis_size("gx"), lax.axis_size("gy")
    groups = [[x * ny + y for x in range(p, nx, 2) for y in range(ny)] for p in (0, 1)]
    return lax.all_to_all(rows, ("gx", "gy"), 0, 0, tiled=True, axis_index_groups=groups)


def per_device(forward_pops, later_adjoint, design, node_type, region):
    far, near = swap(*first_y(forward_pops, later_adjoint, design, node_type), "gy")
    own_up, own_down = first_x(forward_pops, later_adjoint, design, node_type)
    xlow, xhigh = exchange(*join_x(own_up, own_down, far, near), "gx")
    adjoint, raw, part, up, down = main(
        forward_pops, later_adjoint, design, node_type, region, xlow, xhigh, far, near
    )
    xlow, xhigh = exchange(up, down, "gx")
    pairs = lax.axis_size("gx") * lax.axis_size("gy") // 2
    far, near, rows = raw_y(raw, part, xlow, xhigh, pairs)
    rows = share(rows)
    far, near = swap(far, near, "gy")
    sensitivity, objective, volumes = spread(raw, xlow, xhigh, far, near, rows)
    return adjoint, sensitivity, objective[0], volumes


def solution(mesh):
    cells = P("gx", "gy", None)
    pops = P(None, "gx", "gy", None)
    return jax.shard_map(
        per_device,
        mesh=mesh,
        in_specs=(pops, pops, cells, cells, cells),
        out_specs=(pops, cells, P(), P()),
        check_vma=False,
    )
```

```python
import math

import jax
import jax.numpy as jnp
from jax import lax
from jax.experimental import pallas as pl
from jax.experimental.pallas import tpu as pltpu
from jax.sharding import PartitionSpec as P

RAD = 3
REG = 8
VELOCITY = [
    (0, 0, 0),
    (1, 0, 0),
    (-1, 0, 0),
    (0, 1, 0),
    (0, -1, 0),
    (0, 0, 1),
    (0, 0, -1),
    (1, 1, 0),
    (-1, -1, 0),
    (1, -1, 0),
    (-1, 1, 0),
    (1, 0, 1),
    (-1, 0, -1),
    (1, 0, -1),
    (-1, 0, 1),
    (0, 1, 1),
    (0, -1, -1),
    (0, 1, -1),
    (0, -1, 1),
]
WEIGHTS = [1.0 / 3.0] + [1.0 / 18.0] * 6 + [1.0 / 36.0] * 12
OPPOSITE = [0, 2, 1, 4, 3, 6, 5, 8, 7, 10, 9, 12, 11, 14, 13, 16, 15, 18, 17]
RELAXATION = 1.0 / 0.6
BRINKMAN = 0.9
Q = 19
BX = 8
BY = 16
NZ = 128
F32 = jnp.float32


KIND, DENS, MOVING = 0, 1, 5
DEEP = RAD + 2


def sided(axis, sign, ring):
    keep = (lambda c: c >= 0) if ring == 0 else (lambda c: c > 0)
    go = [i for i in range(Q) if keep(sign * VELOCITY[i][axis])]
    come = [i for i in range(Q) if keep(-sign * VELOCITY[i][axis])]
    return go, come


SIZES = [MOVING + sum(map(len, sided(0, 1, ring))) for ring in (0, 1)]
BASES = (0, SIZES[0])
DESIGN = sum(SIZES)
MSG = DESIGN + DEEP
LINE = BY + 4
WIDE_LINE = BY + 2 * DEEP
FLAT = (DESIGN * LINE + DEEP * WIDE_LINE + 7) // 8 * 8
RAW_ROWS = RAD * BY


def design_row(j):
    return DESIGN * LINE + j * WIDE_LINE


def slot(axis, sign, ring, field, which=None):
    base = BASES[ring]
    if field in ("go", "come"):
        go, come = sided(axis, sign, ring)
        listed = go if field == "go" else come
        if which not in listed:
            return None
        return base + MOVING + (0 if field == "go" else len(go)) + listed.index(which)
    return base + field


CLASSES = sorted(
    {a * a + b * b for a in range(RAD + 1) for b in range(RAD + 1) if a * a + b * b < (RAD + 1) ** 2}
)
TAPS = {
    s: [
        (a, b)
        for a in range(-RAD, RAD + 1)
        for b in range(-RAD, RAD + 1)
        if a * a + b * b == s
    ]
    for s in CLASSES
}


def tap_weight(s, c):
    return RAD + 1 - math.sqrt(s + c * c)


def lanes(shape):
    return lax.broadcasted_iota(jnp.int32, shape, len(shape) - 1)


def shift_z(value, c):
    if c == 0:
        return value
    z = lanes(value.shape)
    moved = pltpu.roll(value, (-c) % NZ, value.ndim - 1)
    return jnp.where(z < NZ - c if c > 0 else z >= -c, moved, 0.0)


def norm_row(shape):
    z = lanes(shape)
    result = None
    for c in range(RAD + 1):
        total = sum(len(TAPS[s]) * tap_weight(s, c) for s in CLASSES if tap_weight(s, c) > 0)
        if c == 0:
            result = jnp.full(shape, total, F32)
        else:
            result = result + jnp.where(z >= c, total, 0.0) + jnp.where(z < NZ - c, total, 0.0)
    return result


def fold_rows(wide, folded, starts):
    def plane(x, carry):
        for k, r in enumerate(starts):
            tile = slice(8 * k, 8 * k + 8)
            folded[0, x, tile, :] = wide[x, r : r + 8, :]
            for b in range(1, RAD + 1):
                folded[b, x, tile, :] = wide[x, r + b : r + b + 8, :] + wide[x, r - b : r - b + 8, :]
        return carry

    lax.fori_loop(0, folded.shape[1], plane, 0)


def filter_rows(load):
    sums = [
        add_all(
            load(a, b) for a in range(-RAD, RAD + 1) for b in range(RAD + 1) if a * a + b * b == s
        )
        for s in CLASSES
    ]
    result = None
    for c in range(RAD + 1):
        mixed = None
        for s, part in zip(CLASSES, sums):
            if tap_weight(s, c) > 0:
                term = tap_weight(s, c) * part
                mixed = term if mixed is None else mixed + term
        if c == 0:
            result = mixed
        else:
            result = result + shift_z(mixed, c) + shift_z(mixed, -c)
    return result


def add_all(values):
    values = list(values)
    while len(values) > 1:
        values = [
            values[k] + values[k + 1] if k + 1 < len(values) else values[k]
            for k in range(0, len(values), 2)
        ]
    return values[0]


def moments(p):
    momenta = []
    for a in range(3):
        up = add_all(p[i] for i in range(Q) if VELOCITY[i][a] == 1)
        down = add_all(p[i] for i in range(Q) if VELOCITY[i][a] == -1)
        momenta.append(up - down)
    return add_all(p), momenta


def along(i, vector):
    result = None
    for a in range(3):
        c = VELOCITY[i][a]
        if c == 0:
            continue
        if result is None:
            result = vector[a] if c == 1 else -vector[a]
        else:
            result = result + vector[a] if c == 1 else result - vector[a]
    return result


def post_tiles(which, straight, bounced, density, momenta, node, factor):
    inverse = 1.0 / density
    u = [factor * (m * inverse) for m in momenta]
    rest = 1.0 - 1.5 * (u[0] * u[0] + u[1] * u[1] + u[2] * u[2])
    rate = jnp.where(node <= 1.5, RELAXATION, 1.0)
    keep = 1.0 - rate
    wall = node == 2.0
    scale = rate * density
    scales = {w: w * scale for w in sorted({WEIGHTS[i] for i in which})}
    result = {}
    for i in which:
        a = along(i, u)
        form = rest if a is None else rest + a * (3.0 + 4.5 * a)
        relaxed = keep * straight[i] + scales[WEIGHTS[i]] * form
        result[i] = jnp.where(wall, bounced[i], relaxed)
    return result


def back_tiles(m, density, plain, node, factor):
    u = [factor * q for q in plain]
    rate = jnp.where(node <= 1.5, RELAXATION, 1.0)
    keep = 1.0 - rate
    wall = node == 2.0

    both = {i: m[i] + m[i + 1] for i in range(1, Q, 2)}
    odds = {i: m[i] - m[i + 1] for i in range(1, Q, 2)}
    axis, edge = 1.0 / 18.0, 1.0 / 36.0
    planes = [both[7] + both[9], both[11] + both[13], both[15] + both[17]]
    zero = (1.0 / 3.0) * m[0] + axis * (both[1] + both[3] + both[5])
    zero = zero + edge * (planes[0] + planes[1] + planes[2])
    one = [
        axis * odds[1] + edge * ((odds[7] + odds[9]) + (odds[11] + odds[13])),
        axis * odds[3] + edge * ((odds[7] - odds[9]) + (odds[15] + odds[17])),
        axis * odds[5] + edge * ((odds[11] - odds[13]) + (odds[15] - odds[17])),
    ]
    two = {
        (0, 0): axis * both[1] + edge * (planes[0] + planes[1]),
        (1, 1): axis * both[3] + edge * (planes[0] + planes[2]),
        (2, 2): axis * both[5] + edge * (planes[1] + planes[2]),
        (0, 1): edge * (both[7] - both[9]),
        (0, 2): edge * (both[11] - both[13]),
        (1, 2): edge * (both[15] - both[17]),
    }
    for a, b in ((0, 1), (0, 2), (1, 2)):
        two[b, a] = two[a, b]
    bent = [two[a, 0] * u[0] + two[a, 1] * u[1] + two[a, 2] * u[2] for a in range(3)]
    dot = lambda p, q: p[0] * q[0] + p[1] * q[1] + p[2] * q[2]
    scalar = zero * (1.0 - 1.5 * dot(u, u)) + 3.0 * dot(one, u) + 4.5 * dot(bent, u)
    vector = [3.0 * (one[a] + 3.0 * bent[a] - zero * u[a]) for a in range(3)]
    start = rate * (scalar - dot(vector, u))
    slope = [(rate * factor) * v for v in vector]
    couplings = [start]
    for i in range(1, Q, 2):
        lean = along(i, slope)
        couplings += [start + lean, start - lean]
    result = [jnp.where(wall, m[OPPOSITE[i]], keep * m[i] + couplings[i]) for i in range(Q)]
    gradient = jnp.where(wall, 0.0, rate * density * dot(vector, plain))
    return result, gradient


def whole(shape):
    return pl.BlockSpec(shape, lambda *_: (0,) * len(shape))


def scalar():
    return pl.BlockSpec(memory_space=pltpu.SMEM)


def anywhere():
    return pl.BlockSpec(memory_space=pl.ANY)


def call(body, outs, ins, specs, scratch=(), flops=1, name=None, out_specs=None, vmem=40):
    size = sum(math.prod(o) for o in outs) * 4 + sum(math.prod(x.shape) for x in ins) * 4
    return pl.pallas_call(
        body,
        out_shape=[jax.ShapeDtypeStruct(o, F32) for o in outs],
        grid=(1,),
        in_specs=specs,
        out_specs=out_specs or [whole(o) for o in outs],
        scratch_shapes=list(scratch),
        cost_estimate=pl.CostEstimate(flops=flops, bytes_accessed=size, transcendentals=0),
        compiler_params=pltpu.CompilerParams(vmem_limit_bytes=vmem * 1024 * 1024),
        name=name,
    )(*ins)


def ring_fields(axis, sign, ring, p, node, later):
    density, momenta = moments(p)
    wall = node == 2.0
    go, come = sided(axis, sign, ring)
    fields = [node, density, *momenta]
    fields += [jnp.where(wall, p[OPPOSITE[i]], p[i]) for i in go]
    return fields + [later(i) for i in come]


def first_x_body(fwd, later, des, node, up_out, down_out):
    for out, sign, planes, deep in (
        (up_out, 1, (BX - 1, BX - 2), slice(BX - DEEP, BX)),
        (down_out, -1, (0, 1), slice(0, DEEP)),
    ):
        out[DESIGN:] = des[deep]
        for ring, x in enumerate(planes):
            for h in (0, 8):
                rows = slice(h, h + 8)
                fields = ring_fields(
                    0,
                    sign,
                    ring,
                    [fwd[i, x, rows, :] for i in range(Q)],
                    node[x, rows, :].astype(F32),
                    lambda i, x=x, rows=rows: later[i, x, rows, :],
                )
                for k, value in enumerate(fields):
                    out[BASES[ring] + k, rows, :] = value


def first_x(fwd, later, design, node):
    ins = (fwd, later, design, node)
    return call(
        first_x_body, [(MSG, BY, NZ)] * 2, ins, [whole(x.shape) for x in ins], flops=800000, name="first_x"
    )


def first_y_body(fwd_any, later_any, design, node, far_out, near_out, fwd, later, up_out, down_out, sems):
    copies = [
        pltpu.make_async_copy(source.at[:, :, at : at + 2, :], target.at[:, :, to : to + 2, :], sems.at[k, e])
        for e, (at, to) in enumerate(((0, 0), (BY - 2, 2)))
        for k, (source, target) in enumerate(((fwd_any, fwd), (later_any, later)))
    ]
    for copy in copies:
        copy.start()
    for copy in copies:
        copy.wait()
    for out, sign, lines, deep in (
        (up_out, 1, (BY - 1, BY - 2), range(BY - DEEP, BY)),
        (down_out, -1, (0, 1), range(DEEP)),
    ):
        for k, y in enumerate(deep):
            out[DESIGN + k] = design[:, y, :]
        for ring, y in enumerate(lines):
            fields = ring_fields(
                1,
                sign,
                ring,
                [fwd[i, :, y % 12, :] for i in range(Q)],
                node[:, y, :].astype(F32),
                lambda i, y=y: later[i, :, y % 12, :],
            )
            for k, value in enumerate(fields):
                out[BASES[ring] + k] = value
    by_parity("gy", up_out, down_out, far_out, near_out)


def first_y(fwd, later, design, node):
    block = pltpu.VMEM((Q, BX, 4, NZ), F32)
    return call(
        first_y_body,
        [(MSG, BX, NZ)] * 2,
        (fwd, later, design, node),
        [anywhere(), anywhere(), whole(design.shape), whole(node.shape)],
        scratch=(
            block,
            block,
            pltpu.VMEM((MSG, BX, NZ), F32),
            pltpu.VMEM((MSG, BX, NZ), F32),
            pltpu.SemaphoreType.DMA((2, 2)),
        ),
        flops=800000,
        name="first_y",
        vmem=60,
    )


def odd(axis):
    return lax.rem(lax.axis_index(axis), 2)


def by_parity(axis, up, down, far_out, near_out):
    @pl.when(odd(axis) == 0)
    def _():
        near_out[...] = up[...]
        far_out[...] = down[...]

    @pl.when(odd(axis) == 1)
    def _():
        near_out[...] = down[...]
        far_out[...] = up[...]


def to_sides(axis, far, near, low, high):
    @pl.when(odd(axis) == 0)
    def _():
        high[...] = near[...]
        low[...] = far[...]

    @pl.when(odd(axis) == 1)
    def _():
        low[...] = near[...]
        high[...] = far[...]


def join_x_body(own_up, own_down, far, near, up_out, down_out, low, high):
    to_sides("gy", far, near, low, high)
    for out, own, sign, planes, deep in (
        (up_out, own_up, 1, (BX - 1, BX - 2), range(BX - DEEP, BX)),
        (down_out, own_down, -1, (0, 1), range(DEEP)),
    ):
        out[...] = jnp.zeros_like(out)
        for k, x in enumerate(deep):
            base = design_row(k)
            out[base + DEEP : base + DEEP + BY, :] = own[DESIGN + k]
            for t in range(DEEP):
                out[base + t : base + t + 1, :] = low[DESIGN + t, x : x + 1, :]
                at = base + DEEP + BY + t
                out[at : at + 1, :] = high[DESIGN + t, x : x + 1, :]
        for ring, x in enumerate(planes):
            go, come = sided(0, sign, ring)
            fields = [(f, None) for f in range(MOVING)] + [("go", i) for i in go] + [("come", i) for i in come]
            for k, (field, i) in enumerate(fields):
                base = (BASES[ring] + k) * LINE
                out[base + 2 : base + 2 + BY, :] = own[BASES[ring] + k]
                for source, side, places in ((low, 1, (1, 0)), (high, -1, (2 + BY, 3 + BY))):
                    for other in (0, 1):
                        found = slot(1, side, other, field, i)
                        if found is not None:
                            at = base + places[other]
                            out[at : at + 1, :] = source[found, x : x + 1, :]


def join_x(own_up, own_down, far, near):
    ins = (own_up, own_down, far, near)
    return call(
        join_x_body,
        [(FLAT, NZ)] * 2,
        ins,
        [whole(x.shape) for x in ins],
        scratch=(pltpu.VMEM((MSG, BX, NZ), F32),) * 2,
        flops=80000,
        name="join_x",
    )


EX = BX + 4
ROW = 8
PADY = 32


def main_body(
    fwd, later_any, design, node, region, xlow, xhigh, far, near,
    adjoint_any, raw, part, up_out, down_out,
    ylow, yhigh, wide, folded, kinds, fine, post, later, mid, flow, flux, first, adjoint, sem, sems,
):
    copy = pltpu.make_async_copy(later_any, later.at[:, 2 : 2 + BX, ROW : ROW + BY, :], sem)
    copy.start()
    to_sides("gy", far, near, ylow, yhigh)
    wide[...] = jnp.zeros_like(wide)
    wide[DEEP : DEEP + BX, ROW : ROW + BY, :] = design[...]
    for j in range(DEEP):
        at = design_row(j)
        wide[j, ROW - DEEP : ROW + BY + DEEP, :] = xlow[at : at + WIDE_LINE, :]
        wide[DEEP + BX + j, ROW - DEEP : ROW + BY + DEEP, :] = xhigh[at : at + WIDE_LINE, :]
        for x in range(BX):
            wide[DEEP + x, ROW - DEEP + j : ROW - DEEP + j + 1, :] = ylow[DESIGN + j, x : x + 1, :]
            wide[DEEP + x, ROW + BY + j : ROW + BY + j + 1, :] = yhigh[DESIGN + j, x : x + 1, :]
    long = slice(ROW - 2, ROW + BY + 2)
    xrings = ((1, xlow, 1, 0), (0, xlow, 1, 1), (2 + BX, xhigh, -1, 0), (3 + BX, xhigh, -1, 1))
    yrings = ((ROW - 1, ylow, 1, 0), (ROW - 2, ylow, 1, 1), (ROW + BY, yhigh, -1, 0), (ROW + BY + 1, yhigh, -1, 1))
    kinds[...] = jnp.zeros_like(kinds)
    kinds[2 : 2 + BX, ROW : ROW + BY, :] = node[...].astype(F32)

    def line(message, k):
        return message[k * LINE : (k + 1) * LINE, :]

    for x, message, sign, ring in xrings:
        kinds[x, long, :] = line(message, slot(0, sign, ring, KIND))
    for row, message, sign, ring in yrings:
        for x in range(BX):
            kinds[2 + x, row : row + 1, :] = message[slot(1, sign, ring, KIND), x : x + 1, :]
    inverse_norm = 1.0 / norm_row((8, NZ))

    fold_rows(wide, folded, (4, 12, 20))

    def filter_plane(x, carry):
        for k, r in enumerate((4, 12, 20)):
            tile = slice(8 * k, 8 * k + 8)
            value = filter_rows(lambda a, b: folded[b, x + RAD + a, tile, :]) * inverse_norm
            fine[x, r : r + 8, :] = value
        return carry

    lax.fori_loop(0, EX, filter_plane, 0)

    def factor_of(kind, filtered):
        return jnp.where(kind == 1.0, 1.0 - BRINKMAN * (1.0 - filtered), 1.0)

    for x, message, sign, ring in xrings:
        comps = sided(0, sign, ring)[0]
        kind = kinds[x, long, :]
        q = {i: line(message, slot(0, sign, ring, "go", i)) for i in comps}
        base = slot(0, sign, ring, DENS)
        value = post_tiles(
            comps, q, q, line(message, base), [line(message, base + 1 + a) for a in range(3)],
            kind, factor_of(kind, fine[x, long, :]),
        )
        for i in comps:
            post[i, x, long, :] = value[i]
    for row, message, sign, ring in yrings:
        comps = sided(1, sign, ring)[0]
        kind = kinds[2 : 2 + BX, row, :]
        q = {i: message[slot(1, sign, ring, "go", i)] for i in comps}
        base = slot(1, sign, ring, DENS)
        value = post_tiles(
            comps, q, q, message[base], [message[base + 1 + a] for a in range(3)],
            kind, factor_of(kind, fine[2 : 2 + BX, row, :]),
        )
        for i in comps:
            for x in range(BX):
                post[i, 2 + x, row : row + 1, :] = value[i][x : x + 1, :]

    def post_plane(x, carry):
        carry = list(carry)
        for h in (0, 8):
            rows = slice(h, h + 8)
            padded = slice(ROW + h, ROW + h + 8)
            p = [fwd[i, x, rows, :] for i in range(Q)]
            density, momenta = moments(p)
            kind = kinds[x + 2, padded, :]
            filtered = fine[x + 2, padded, :]
            inverse = 1.0 / density
            flow[0, x, rows, :] = density
            for a in range(3):
                flow[1 + a, x, rows, :] = momenta[a] * inverse
            bounced = [p[OPPOSITE[i]] for i in range(Q)]
            value = post_tiles(range(Q), p, bounced, density, momenta, kind, factor_of(kind, filtered))
            for i in range(Q):
                post[i, x + 2, padded, :] = value[i]
            counted = jnp.where(kind == 1.0, filtered, 0.0)
            where_region = region[x, rows, :]
            for r in range(REG):
                carry[r] = carry[r] + jnp.where(where_region == r, counted, 0.0)
        return tuple(carry)

    empty = jnp.zeros((8, NZ), F32)
    totals = lax.fori_loop(0, BX, post_plane, (empty,) * REG)
    copy.wait()
    for x, message, sign, ring in xrings:
        for i in sided(0, sign, ring)[1]:
            later[i, x, long, :] = line(message, slot(0, sign, ring, "come", i))
    for row, message, sign, ring in yrings:
        for i in sided(1, sign, ring)[1]:
            found = slot(1, sign, ring, "come", i)
            for x in range(BX):
                later[i, 2 + x, row : row + 1, :] = message[found, x : x + 1, :]

    def mid_plane(x, carry):
        for start in (ROW - 1, ROW + 7, ROW + 15):
            rows = slice(start, start + 8)
            density, mx, my, mz = 0.0, 0.0, 0.0, 0.0
            for cz in (0, 1, -1):
                p = {}
                for i in range(Q):
                    if VELOCITY[i][2] == cz:
                        at = start - VELOCITY[i][1]
                        p[i] = post[i, x + 1 - VELOCITY[i][0], at : at + 8, :]
                whole_sum = shift_z(add_all(p.values()), -cz)
                density = density + whole_sum
                if cz:
                    mz = mz + cz * whole_sum
                sides = []
                for a in range(2):
                    up = add_all(p[i] for i in p if VELOCITY[i][a] == 1)
                    down = add_all(p[i] for i in p if VELOCITY[i][a] == -1)
                    sides.append(shift_z(up - down, -cz))
                mx = mx + sides[0]
                my = my + sides[1]
            kind = kinds[x + 1, rows, :]
            outlet = kind == 4.0
            flux[x, rows, :] = jnp.where(outlet, mx, 0.0)
            inverse = 1.0 / density
            m = []
            for i in range(Q):
                at = start + VELOCITY[i][1]
                m.append(shift_z(later[i, x + 1 + VELOCITY[i][0], at : at + 8, :], VELOCITY[i][2]))
            value, gradient = back_tiles(
                m, density, [mx * inverse, my * inverse, mz * inverse], kind,
                factor_of(kind, fine[x + 1, rows, :]),
            )
            source = jnp.where(outlet, 1.0, 0.0)
            for i in range(Q):
                c = VELOCITY[i][0]
                mid[i, x, rows, :] = value[i] + c * source if c else value[i]
            first[x, rows, :] = gradient
        return carry

    lax.fori_loop(0, BX + 2, mid_plane, 0)
    raw_scale = BRINKMAN * inverse_norm

    def send(x):
        at = pl.ds(x, 1)
        return pltpu.make_async_copy(adjoint.at[:, at], adjoint_any.at[:, at], sems.at[x])

    def last_plane(x, carry):
        for h in (0, 8):
            rows = slice(h, h + 8)
            padded = slice(ROW + h, ROW + h + 8)
            kind = kinds[x + 2, padded, :]
            carry = carry + flux[x + 1, padded, :]
            m = []
            for i in range(Q):
                at = ROW + h + VELOCITY[i][1]
                m.append(shift_z(mid[i, x + 1 + VELOCITY[i][0], at : at + 8, :], VELOCITY[i][2]))
            value, gradient = back_tiles(
                m, flow[0, x, rows, :], [flow[1 + a, x, rows, :] for a in range(3)], kind,
                factor_of(kind, fine[x + 2, padded, :]),
            )
            for i in range(Q):
                adjoint[i, x, rows, :] = value[i]
            both = (first[x + 1, padded, :] + gradient) * raw_scale
            raw[x, rows, :] = jnp.where(kind == 1.0, both, 0.0)
        send(x).start()
        return carry

    totals = (*totals, lax.fori_loop(0, BX, last_plane, empty))
    row = jnp.zeros((8, NZ), F32)
    for r, value in enumerate(totals):
        row = jnp.where(lanes((8, NZ)) == r, jnp.sum(value, axis=(0, 1), keepdims=True), row)
    part[...] = row
    for out, begin in ((up_out, BX - RAD), (down_out, 0)):
        for j in range(RAD):
            out[j * BY : (j + 1) * BY, :] = raw[begin + j]
        out[RAW_ROWS:, :] = row
    for x in range(BX):
        send(x).wait()


def main(fwd, later, design, node, region, xlow, xhigh, far, near):
    ins = (fwd, later, design, node, region, xlow, xhigh, far, near)
    specs = [whole(x.shape) for x in ins]
    specs[1] = anywhere()
    outs = [(Q, BX, BY, NZ), (BX, BY, NZ), (8, NZ), (RAW_ROWS + 8, NZ), (RAW_ROWS + 8, NZ)]
    return call(
        main_body,
        outs,
        ins,
        specs,
        scratch=(
            pltpu.VMEM((MSG, BX, NZ), F32),
            pltpu.VMEM((MSG, BX, NZ), F32),
            pltpu.VMEM((BX + 2 * DEEP, PADY, NZ), F32),
            pltpu.VMEM((RAD + 1, BX + 2 * DEEP, 24, NZ), F32),
            pltpu.VMEM((EX, PADY, NZ), F32),
            pltpu.VMEM((EX, PADY, NZ), F32),
            pltpu.VMEM((Q, EX, PADY, NZ), F32),
            pltpu.VMEM((Q, EX, PADY, NZ), F32),
            pltpu.VMEM((Q, BX + 2, PADY, NZ), F32),
            pltpu.VMEM((4, BX, BY, NZ), F32),
            pltpu.VMEM((BX + 2, PADY, NZ), F32),
            pltpu.VMEM((BX + 2, PADY, NZ), F32),
            pltpu.VMEM((Q, BX, BY, NZ), F32),
            pltpu.SemaphoreType.DMA,
            pltpu.SemaphoreType.DMA((BX,)),
        ),
        flops=30000000,
        name="main",
        out_specs=[anywhere()] + [whole(o) for o in outs[1:]],
    )


def raw_y_body(raw, part, low, high, far_out, near_out, rows_out, up_out, down_out):
    for out, begin in ((up_out, BY - RAD), (down_out, 0)):
        out[...] = jnp.zeros_like(out)
        for j in range(RAD):
            y = begin + j
            out[j, RAD : RAD + BX, :] = raw[:, y, :]
            for x in range(RAD):
                out[j, x : x + 1, :] = low[x * BY + y : x * BY + y + 1, :]
                out[j, RAD + BX + x : RAD + BX + x + 1, :] = high[x * BY + y : x * BY + y + 1, :]
    by_parity("gy", up_out, down_out, far_out, near_out)
    other = jnp.where(odd("gx") == 1, low[RAW_ROWS : RAW_ROWS + 8, :], high[RAW_ROWS : RAW_ROWS + 8, :])
    row = part[...] + other
    for k in range(0, rows_out.shape[0], 8):
        rows_out[k : k + 8, :] = row


def raw_y(raw, part, low, high, count):
    ins = (raw, part, low, high)
    return call(
        raw_y_body,
        [(RAD, BY, NZ), (RAD, BY, NZ), (count, NZ)],
        ins,
        [whole(x.shape) for x in ins],
        scratch=(pltpu.VMEM((RAD, BY, NZ), F32),) * 2,
        flops=20000,
        name="raw_y",
    )


def spread_body(raw, xlow, xhigh, far, near, rows, out, objective, volumes, ylow, yhigh, wide, folded):
    to_sides("gy", far, near, ylow, yhigh)
    wide[RAD : RAD + BX, ROW : ROW + BY, :] = raw[...]
    for j in range(RAD):
        wide[j, ROW : ROW + BY, :] = xlow[j * BY : (j + 1) * BY, :]
        wide[RAD + BX + j, ROW : ROW + BY, :] = xhigh[j * BY : (j + 1) * BY, :]
    for x in range(BX + 2 * RAD):
        for j in range(RAD):
            wide[x, ROW - RAD + j : ROW - RAD + j + 1, :] = ylow[j, x : x + 1, :]
            wide[x, ROW + BY + j : ROW + BY + j + 1, :] = yhigh[j, x : x + 1, :]

    fold_rows(wide, folded, (ROW, ROW + 8))

    def plane(x, carry):
        for h in (0, 8):
            out[x, h : h + 8, :] = filter_rows(lambda a, b: folded[b, x + RAD + a, h : h + 8, :])
        return carry

    lax.fori_loop(0, BX, plane, 0)
    total = add_all(rows[k : k + 8, :] for k in range(0, rows.shape[0], 8))
    lane = lanes((8, NZ))
    for r in range(REG + 1):
        value = jnp.sum(jnp.where(lane == r, total, 0.0))
        if r < REG:
            volumes[r] = value
        else:
            objective[0] = value


def spread(raw, xlow, xhigh, far, near, rows):
    ins = (raw, xlow, xhigh, far, near, rows)
    return call(
        spread_body,
        [(BX, BY, NZ), (1,), (REG,)],
        ins,
        [whole(x.shape) for x in ins],
        scratch=(pltpu.VMEM((RAD, BY, NZ), F32),) * 2
        + (pltpu.VMEM((BX + 2 * RAD, PADY, NZ), F32), pltpu.VMEM((RAD + 1, BX + 2 * RAD, BY, NZ), F32)),
        flops=2000000,
        name="spread",
        out_specs=[whole((BX, BY, NZ)), scalar(), scalar()],
    )


def exchange(up, down, axis):
    count = lax.axis_size(axis)
    forward = [(i, (i + 1) % count) for i in range(count)]
    backward = [(j, i) for i, j in forward]
    return lax.ppermute(up, axis, forward), lax.ppermute(down, axis, backward)


def swap(far, near, axis):
    count = lax.axis_size(axis)
    inner = [(i, i ^ 1) for i in range(count)]
    outer = [(i, (i + 1 if i % 2 else i - 1) % count) for i in range(count)]
    return lax.ppermute(far, axis, outer), lax.ppermute(near, axis, inner)


def share(rows):
    nx, ny = lax.axis_size("gx"), lax.axis_size("gy")
    groups = [[x * ny + y for x in range(p, nx, 2) for y in range(ny)] for p in (0, 1)]
    return lax.all_to_all(rows, ("gx", "gy"), 0, 0, tiled=True, axis_index_groups=groups)


def per_device(forward_pops, later_adjoint, design, node_type, region):
    far, near = swap(*first_y(forward_pops, later_adjoint, design, node_type), "gy")
    own_up, own_down = first_x(forward_pops, later_adjoint, design, node_type)
    xlow, xhigh = exchange(*join_x(own_up, own_down, far, near), "gx")
    adjoint, raw, part, up, down = main(
        forward_pops, later_adjoint, design, node_type, region, xlow, xhigh, far, near
    )
    xlow, xhigh = exchange(up, down, "gx")
    pairs = lax.axis_size("gx") * lax.axis_size("gy") // 2
    far, near, rows = raw_y(raw, part, xlow, xhigh, pairs)
    rows = share(rows)
    far, near = swap(far, near, "gy")
    sensitivity, objective, volumes = spread(raw, xlow, xhigh, far, near, rows)
    return adjoint, sensitivity, objective[0], volumes


def solution(mesh):
    cells = P("gx", "gy", None)
    pops = P(None, "gx", "gy", None)
    return jax.shard_map(
        per_device,
        mesh=mesh,
        in_specs=(pops, pops, cells, cells, cells),
        out_specs=(pops, cells, P(), P()),
        check_vma=False,
    )
```

```python
import math

import jax
import jax.numpy as jnp
from jax import lax
from jax.experimental import pallas as pl
from jax.experimental.pallas import tpu as pltpu
from jax.sharding import PartitionSpec as P

RAD = 3
REG = 8
VELOCITY = [
    (0, 0, 0),
    (1, 0, 0),
    (-1, 0, 0),
    (0, 1, 0),
    (0, -1, 0),
    (0, 0, 1),
    (0, 0, -1),
    (1, 1, 0),
    (-1, -1, 0),
    (1, -1, 0),
    (-1, 1, 0),
    (1, 0, 1),
    (-1, 0, -1),
    (1, 0, -1),
    (-1, 0, 1),
    (0, 1, 1),
    (0, -1, -1),
    (0, 1, -1),
    (0, -1, 1),
]
WEIGHTS = [1.0 / 3.0] + [1.0 / 18.0] * 6 + [1.0 / 36.0] * 12
OPPOSITE = [0, 2, 1, 4, 3, 6, 5, 8, 7, 10, 9, 12, 11, 14, 13, 16, 15, 18, 17]
RELAXATION = 1.0 / 0.6
BRINKMAN = 0.9
Q = 19
BX = 8
BY = 16
NZ = 128
F32 = jnp.float32


KIND, DENS, MOVING = 0, 1, 5
DEEP = RAD + 2


def sided(axis, sign, ring):
    keep = (lambda c: c >= 0) if ring == 0 else (lambda c: c > 0)
    go = [i for i in range(Q) if keep(sign * VELOCITY[i][axis])]
    come = [i for i in range(Q) if keep(-sign * VELOCITY[i][axis])]
    return go, come


SIZES = [MOVING + sum(map(len, sided(0, 1, ring))) for ring in (0, 1)]
BASES = (0, SIZES[0])
DESIGN = sum(SIZES)
MSG = DESIGN + DEEP
LINE = BY + 4
WIDE_LINE = BY + 2 * DEEP
FLAT = (DESIGN * LINE + DEEP * WIDE_LINE + 7) // 8 * 8
RAW_ROWS = RAD * BY


def design_row(j):
    return DESIGN * LINE + j * WIDE_LINE


def slot(axis, sign, ring, field, which=None):
    base = BASES[ring]
    if field in ("go", "come"):
        go, come = sided(axis, sign, ring)
        listed = go if field == "go" else come
        if which not in listed:
            return None
        return base + MOVING + (0 if field == "go" else len(go)) + listed.index(which)
    return base + field


CLASSES = sorted(
    {a * a + b * b for a in range(RAD + 1) for b in range(RAD + 1) if a * a + b * b < (RAD + 1) ** 2}
)
TAPS = {
    s: [
        (a, b)
        for a in range(-RAD, RAD + 1)
        for b in range(-RAD, RAD + 1)
        if a * a + b * b == s
    ]
    for s in CLASSES
}


def tap_weight(s, c):
    return RAD + 1 - math.sqrt(s + c * c)


def lanes(shape):
    return lax.broadcasted_iota(jnp.int32, shape, len(shape) - 1)


def shift_z(value, c):
    if c == 0:
        return value
    z = lanes(value.shape)
    moved = pltpu.roll(value, (-c) % NZ, value.ndim - 1)
    return jnp.where(z < NZ - c if c > 0 else z >= -c, moved, 0.0)


def norm_row(shape):
    z = lanes(shape)
    result = None
    for c in range(RAD + 1):
        total = sum(len(TAPS[s]) * tap_weight(s, c) for s in CLASSES if tap_weight(s, c) > 0)
        if c == 0:
            result = jnp.full(shape, total, F32)
        else:
            result = result + jnp.where(z >= c, total, 0.0) + jnp.where(z < NZ - c, total, 0.0)
    return result


def fold_rows(wide, folded, starts):
    def plane(x, carry):
        for k, r in enumerate(starts):
            tile = slice(8 * k, 8 * k + 8)
            folded[0, x, tile, :] = wide[x, r : r + 8, :]
            for b in range(1, RAD + 1):
                folded[b, x, tile, :] = wide[x, r + b : r + b + 8, :] + wide[x, r - b : r - b + 8, :]
        return carry

    lax.fori_loop(0, folded.shape[1], plane, 0)


def filter_rows(load):
    sums = [
        add_all(
            load(a, b) for a in range(-RAD, RAD + 1) for b in range(RAD + 1) if a * a + b * b == s
        )
        for s in CLASSES
    ]
    result = None
    for c in range(RAD + 1):
        mixed = None
        for s, part in zip(CLASSES, sums):
            if tap_weight(s, c) > 0:
                term = tap_weight(s, c) * part
                mixed = term if mixed is None else mixed + term
        if c == 0:
            result = mixed
        else:
            result = result + shift_z(mixed, c) + shift_z(mixed, -c)
    return result


def add_all(values):
    values = list(values)
    while len(values) > 1:
        values = [
            values[k] + values[k + 1] if k + 1 < len(values) else values[k]
            for k in range(0, len(values), 2)
        ]
    return values[0]


def moments(p):
    momenta = []
    for a in range(3):
        up = add_all(p[i] for i in range(Q) if VELOCITY[i][a] == 1)
        down = add_all(p[i] for i in range(Q) if VELOCITY[i][a] == -1)
        momenta.append(up - down)
    return add_all(p), momenta


def along(i, vector):
    result = None
    for a in range(3):
        c = VELOCITY[i][a]
        if c == 0:
            continue
        if result is None:
            result = vector[a] if c == 1 else -vector[a]
        else:
            result = result + vector[a] if c == 1 else result - vector[a]
    return result


def post_tiles(which, straight, bounced, density, momenta, node, factor):
    inverse = 1.0 / density
    u = [factor * (m * inverse) for m in momenta]
    rest = 1.0 - 1.5 * (u[0] * u[0] + u[1] * u[1] + u[2] * u[2])
    rate = jnp.where(node <= 1.5, RELAXATION, 1.0)
    keep = 1.0 - rate
    wall = node == 2.0
    scale = rate * density
    scales = {w: w * scale for w in sorted({WEIGHTS[i] for i in which})}
    result = {}
    for i in which:
        a = along(i, u)
        form = rest if a is None else rest + a * (3.0 + 4.5 * a)
        relaxed = keep * straight[i] + scales[WEIGHTS[i]] * form
        result[i] = jnp.where(wall, bounced[i], relaxed)
    return result


def back_tiles(m, density, plain, node, factor):
    u = [factor * q for q in plain]
    rate = jnp.where(node <= 1.5, RELAXATION, 1.0)
    keep = 1.0 - rate
    wall = node == 2.0

    both = {i: m[i] + m[i + 1] for i in range(1, Q, 2)}
    odds = {i: m[i] - m[i + 1] for i in range(1, Q, 2)}
    axis, edge = 1.0 / 18.0, 1.0 / 36.0
    planes = [both[7] + both[9], both[11] + both[13], both[15] + both[17]]
    zero = (1.0 / 3.0) * m[0] + axis * (both[1] + both[3] + both[5])
    zero = zero + edge * (planes[0] + planes[1] + planes[2])
    one = [
        axis * odds[1] + edge * ((odds[7] + odds[9]) + (odds[11] + odds[13])),
        axis * odds[3] + edge * ((odds[7] - odds[9]) + (odds[15] + odds[17])),
        axis * odds[5] + edge * ((odds[11] - odds[13]) + (odds[15] - odds[17])),
    ]
    two = {
        (0, 0): axis * both[1] + edge * (planes[0] + planes[1]),
        (1, 1): axis * both[3] + edge * (planes[0] + planes[2]),
        (2, 2): axis * both[5] + edge * (planes[1] + planes[2]),
        (0, 1): edge * (both[7] - both[9]),
        (0, 2): edge * (both[11] - both[13]),
        (1, 2): edge * (both[15] - both[17]),
    }
    for a, b in ((0, 1), (0, 2), (1, 2)):
        two[b, a] = two[a, b]
    bent = [two[a, 0] * u[0] + two[a, 1] * u[1] + two[a, 2] * u[2] for a in range(3)]
    dot = lambda p, q: p[0] * q[0] + p[1] * q[1] + p[2] * q[2]
    scalar = zero * (1.0 - 1.5 * dot(u, u)) + 3.0 * dot(one, u) + 4.5 * dot(bent, u)
    vector = [3.0 * (one[a] + 3.0 * bent[a] - zero * u[a]) for a in range(3)]
    start = rate * (scalar - dot(vector, u))
    slope = [(rate * factor) * v for v in vector]
    couplings = [start]
    for i in range(1, Q, 2):
        lean = along(i, slope)
        couplings += [start + lean, start - lean]
    result = [jnp.where(wall, m[OPPOSITE[i]], keep * m[i] + couplings[i]) for i in range(Q)]
    gradient = jnp.where(wall, 0.0, rate * density * dot(vector, plain))
    return result, gradient


def whole(shape):
    return pl.BlockSpec(shape, lambda *_: (0,) * len(shape))


def scalar():
    return pl.BlockSpec(memory_space=pltpu.SMEM)


def anywhere():
    return pl.BlockSpec(memory_space=pl.ANY)


def call(body, outs, ins, specs, scratch=(), flops=1, name=None, out_specs=None, vmem=40):
    size = sum(math.prod(o) for o in outs) * 4 + sum(math.prod(x.shape) for x in ins) * 4
    return pl.pallas_call(
        body,
        out_shape=[jax.ShapeDtypeStruct(o, F32) for o in outs],
        grid=(1,),
        in_specs=specs,
        out_specs=out_specs or [whole(o) for o in outs],
        scratch_shapes=list(scratch),
        cost_estimate=pl.CostEstimate(flops=flops, bytes_accessed=size, transcendentals=0),
        compiler_params=pltpu.CompilerParams(vmem_limit_bytes=vmem * 1024 * 1024),
        name=name,
    )(*ins)


def ring_fields(axis, sign, ring, p, node, later):
    density, momenta = moments(p)
    wall = node == 2.0
    go, come = sided(axis, sign, ring)
    fields = [node, density, *momenta]
    fields += [jnp.where(wall, p[OPPOSITE[i]], p[i]) for i in go]
    return fields + [later(i) for i in come]


def first_x_body(fwd, later, des, node, up_out, down_out):
    for out, sign, planes, deep in (
        (up_out, 1, (BX - 1, BX - 2), slice(BX - DEEP, BX)),
        (down_out, -1, (0, 1), slice(0, DEEP)),
    ):
        out[DESIGN:] = des[deep]
        for ring, x in enumerate(planes):
            for h in (0, 8):
                rows = slice(h, h + 8)
                fields = ring_fields(
                    0,
                    sign,
                    ring,
                    [fwd[i, x, rows, :] for i in range(Q)],
                    node[x, rows, :].astype(F32),
                    lambda i, x=x, rows=rows: later[i, x, rows, :],
                )
                for k, value in enumerate(fields):
                    out[BASES[ring] + k, rows, :] = value


def first_x(fwd, later, design, node):
    ins = (fwd, later, design, node)
    return call(
        first_x_body, [(MSG, BY, NZ)] * 2, ins, [whole(x.shape) for x in ins], flops=800000, name="first_x"
    )


def first_y_body(fwd_any, later_any, design, node, far_out, near_out, fwd, later, up_out, down_out, sems):
    copies = [
        pltpu.make_async_copy(source.at[:, :, at : at + 2, :], target.at[:, :, to : to + 2, :], sems.at[k, e])
        for e, (at, to) in enumerate(((0, 0), (BY - 2, 2)))
        for k, (source, target) in enumerate(((fwd_any, fwd), (later_any, later)))
    ]
    for copy in copies:
        copy.start()
    for copy in copies:
        copy.wait()
    for out, sign, lines, deep in (
        (up_out, 1, (BY - 1, BY - 2), range(BY - DEEP, BY)),
        (down_out, -1, (0, 1), range(DEEP)),
    ):
        for k, y in enumerate(deep):
            out[DESIGN + k] = design[:, y, :]
        for ring, y in enumerate(lines):
            fields = ring_fields(
                1,
                sign,
                ring,
                [fwd[i, :, y % 12, :] for i in range(Q)],
                node[:, y, :].astype(F32),
                lambda i, y=y: later[i, :, y % 12, :],
            )
            for k, value in enumerate(fields):
                out[BASES[ring] + k] = value
    by_parity("gy", up_out, down_out, far_out, near_out)


def first_y(fwd, later, design, node):
    block = pltpu.VMEM((Q, BX, 4, NZ), F32)
    return call(
        first_y_body,
        [(MSG, BX, NZ)] * 2,
        (fwd, later, design, node),
        [anywhere(), anywhere(), whole(design.shape), whole(node.shape)],
        scratch=(
            block,
            block,
            pltpu.VMEM((MSG, BX, NZ), F32),
            pltpu.VMEM((MSG, BX, NZ), F32),
            pltpu.SemaphoreType.DMA((2, 2)),
        ),
        flops=800000,
        name="first_y",
        vmem=60,
    )


def odd(axis):
    return lax.rem(lax.axis_index(axis), 2)


def by_parity(axis, up, down, far_out, near_out):
    @pl.when(odd(axis) == 0)
    def _():
        near_out[...] = up[...]
        far_out[...] = down[...]

    @pl.when(odd(axis) == 1)
    def _():
        near_out[...] = down[...]
        far_out[...] = up[...]


def to_sides(axis, far, near, low, high):
    @pl.when(odd(axis) == 0)
    def _():
        high[...] = near[...]
        low[...] = far[...]

    @pl.when(odd(axis) == 1)
    def _():
        low[...] = near[...]
        high[...] = far[...]


def join_x_body(own_up, own_down, far, near, up_out, down_out, low, high):
    to_sides("gy", far, near, low, high)
    for out, own, sign, planes, deep in (
        (up_out, own_up, 1, (BX - 1, BX - 2), range(BX - DEEP, BX)),
        (down_out, own_down, -1, (0, 1), range(DEEP)),
    ):
        out[...] = jnp.zeros_like(out)
        for k, x in enumerate(deep):
            base = design_row(k)
            out[base + DEEP : base + DEEP + BY, :] = own[DESIGN + k]
            for t in range(DEEP):
                out[base + t : base + t + 1, :] = low[DESIGN + t, x : x + 1, :]
                at = base + DEEP + BY + t
                out[at : at + 1, :] = high[DESIGN + t, x : x + 1, :]
        for ring, x in enumerate(planes):
            go, come = sided(0, sign, ring)
            fields = [(f, None) for f in range(MOVING)] + [("go", i) for i in go] + [("come", i) for i in come]
            for k, (field, i) in enumerate(fields):
                base = (BASES[ring] + k) * LINE
                out[base + 2 : base + 2 + BY, :] = own[BASES[ring] + k]
                for source, side, places in ((low, 1, (1, 0)), (high, -1, (2 + BY, 3 + BY))):
                    for other in (0, 1):
                        found = slot(1, side, other, field, i)
                        if found is not None:
                            at = base + places[other]
                            out[at : at + 1, :] = source[found, x : x + 1, :]


def join_x(own_up, own_down, far, near):
    ins = (own_up, own_down, far, near)
    return call(
        join_x_body,
        [(FLAT, NZ)] * 2,
        ins,
        [whole(x.shape) for x in ins],
        scratch=(pltpu.VMEM((MSG, BX, NZ), F32),) * 2,
        flops=80000,
        name="join_x",
    )


EX = BX + 4
ROW = 8
PADY = 32


def main_body(
    fwd, later_any, design, node, region, xlow, xhigh, far, near,
    adjoint_any, raw, part, up_out, down_out,
    ylow, yhigh, wide, folded, kinds, fine, post, later, mid, flow, flux, first, adjoint, sem, sems,
):
    copy = pltpu.make_async_copy(later_any, later.at[:, 2 : 2 + BX, ROW : ROW + BY, :], sem)
    copy.start()
    to_sides("gy", far, near, ylow, yhigh)
    wide[...] = jnp.zeros_like(wide)
    wide[DEEP : DEEP + BX, ROW : ROW + BY, :] = design[...]
    for j in range(DEEP):
        at = design_row(j)
        wide[j, ROW - DEEP : ROW + BY + DEEP, :] = xlow[at : at + WIDE_LINE, :]
        wide[DEEP + BX + j, ROW - DEEP : ROW + BY + DEEP, :] = xhigh[at : at + WIDE_LINE, :]
        for x in range(BX):
            wide[DEEP + x, ROW - DEEP + j : ROW - DEEP + j + 1, :] = ylow[DESIGN + j, x : x + 1, :]
            wide[DEEP + x, ROW + BY + j : ROW + BY + j + 1, :] = yhigh[DESIGN + j, x : x + 1, :]
    long = slice(ROW - 2, ROW + BY + 2)
    xrings = ((1, xlow, 1, 0), (0, xlow, 1, 1), (2 + BX, xhigh, -1, 0), (3 + BX, xhigh, -1, 1))
    yrings = ((ROW - 1, ylow, 1, 0), (ROW - 2, ylow, 1, 1), (ROW + BY, yhigh, -1, 0), (ROW + BY + 1, yhigh, -1, 1))
    kinds[...] = jnp.zeros_like(kinds)
    kinds[2 : 2 + BX, ROW : ROW + BY, :] = node[...].astype(F32)

    def line(message, k):
        return message[k * LINE : (k + 1) * LINE, :]

    for x, message, sign, ring in xrings:
        kinds[x, long, :] = line(message, slot(0, sign, ring, KIND))
    for row, message, sign, ring in yrings:
        for x in range(BX):
            kinds[2 + x, row : row + 1, :] = message[slot(1, sign, ring, KIND), x : x + 1, :]
    inverse_norm = 1.0 / norm_row((8, NZ))

    fold_rows(wide, folded, (4, 12, 20))

    def filter_plane(x, carry):
        for k, r in enumerate((4, 12, 20)):
            tile = slice(8 * k, 8 * k + 8)
            value = filter_rows(lambda a, b: folded[b, x + RAD + a, tile, :]) * inverse_norm
            fine[x, r : r + 8, :] = value
        return carry

    lax.fori_loop(0, EX, filter_plane, 0)

    def factor_of(kind, filtered):
        return jnp.where(kind == 1.0, 1.0 - BRINKMAN * (1.0 - filtered), 1.0)

    for x, message, sign, ring in xrings:
        comps = sided(0, sign, ring)[0]
        kind = kinds[x, long, :]
        q = {i: line(message, slot(0, sign, ring, "go", i)) for i in comps}
        base = slot(0, sign, ring, DENS)
        value = post_tiles(
            comps, q, q, line(message, base), [line(message, base + 1 + a) for a in range(3)],
            kind, factor_of(kind, fine[x, long, :]),
        )
        for i in comps:
            post[i, x, long, :] = value[i]
    for row, message, sign, ring in yrings:
        comps = sided(1, sign, ring)[0]
        kind = kinds[2 : 2 + BX, row, :]
        q = {i: message[slot(1, sign, ring, "go", i)] for i in comps}
        base = slot(1, sign, ring, DENS)
        value = post_tiles(
            comps, q, q, message[base], [message[base + 1 + a] for a in range(3)],
            kind, factor_of(kind, fine[2 : 2 + BX, row, :]),
        )
        for i in comps:
            for x in range(BX):
                post[i, 2 + x, row : row + 1, :] = value[i][x : x + 1, :]

    def post_plane(x, carry):
        carry = list(carry)
        for h in (0, 8):
            rows = slice(h, h + 8)
            padded = slice(ROW + h, ROW + h + 8)
            p = [fwd[i, x, rows, :] for i in range(Q)]
            density, momenta = moments(p)
            kind = kinds[x + 2, padded, :]
            filtered = fine[x + 2, padded, :]
            inverse = 1.0 / density
            flow[0, x, rows, :] = density
            for a in range(3):
                flow[1 + a, x, rows, :] = momenta[a] * inverse
            bounced = [p[OPPOSITE[i]] for i in range(Q)]
            value = post_tiles(range(Q), p, bounced, density, momenta, kind, factor_of(kind, filtered))
            for i in range(Q):
                post[i, x + 2, padded, :] = value[i]
            counted = jnp.where(kind == 1.0, filtered, 0.0)
            where_region = region[x, rows, :]
            for r in range(REG):
                carry[r] = carry[r] + jnp.where(where_region == r, counted, 0.0)
        return tuple(carry)

    empty = jnp.zeros((8, NZ), F32)
    totals = lax.fori_loop(0, BX, post_plane, (empty,) * REG)
    copy.wait()
    for x, message, sign, ring in xrings:
        for i in sided(0, sign, ring)[1]:
            later[i, x, long, :] = line(message, slot(0, sign, ring, "come", i))
    for row, message, sign, ring in yrings:
        for i in sided(1, sign, ring)[1]:
            found = slot(1, sign, ring, "come", i)
            for x in range(BX):
                later[i, 2 + x, row : row + 1, :] = message[found, x : x + 1, :]

    def mid_plane(x, carry):
        for start in (ROW - 1, ROW + 7, ROW + 15):
            rows = slice(start, start + 8)
            density, mx, my, mz = 0.0, 0.0, 0.0, 0.0
            for cz in (0, 1, -1):
                p = {}
                for i in range(Q):
                    if VELOCITY[i][2] == cz:
                        at = start - VELOCITY[i][1]
                        p[i] = post[i, x + 1 - VELOCITY[i][0], at : at + 8, :]
                whole_sum = shift_z(add_all(p.values()), -cz)
                density = density + whole_sum
                if cz:
                    mz = mz + cz * whole_sum
                sides = []
                for a in range(2):
                    up = add_all(p[i] for i in p if VELOCITY[i][a] == 1)
                    down = add_all(p[i] for i in p if VELOCITY[i][a] == -1)
                    sides.append(shift_z(up - down, -cz))
                mx = mx + sides[0]
                my = my + sides[1]
            kind = kinds[x + 1, rows, :]
            outlet = kind == 4.0
            flux[x, rows, :] = jnp.where(outlet, mx, 0.0)
            inverse = 1.0 / density
            m = []
            for i in range(Q):
                at = start + VELOCITY[i][1]
                m.append(shift_z(later[i, x + 1 + VELOCITY[i][0], at : at + 8, :], VELOCITY[i][2]))
            value, gradient = back_tiles(
                m, density, [mx * inverse, my * inverse, mz * inverse], kind,
                factor_of(kind, fine[x + 1, rows, :]),
            )
            source = jnp.where(outlet, 1.0, 0.0)
            for i in range(Q):
                c = VELOCITY[i][0]
                mid[i, x, rows, :] = value[i] + c * source if c else value[i]
            first[x, rows, :] = gradient
        return carry

    lax.fori_loop(0, BX + 2, mid_plane, 0)
    raw_scale = BRINKMAN * inverse_norm

    def send(x):
        at = pl.ds(x, 1)
        return pltpu.make_async_copy(adjoint.at[:, at], adjoint_any.at[:, at], sems.at[x])

    def last_plane(x, carry):
        for h in (0, 8):
            rows = slice(h, h + 8)
            padded = slice(ROW + h, ROW + h + 8)
            kind = kinds[x + 2, padded, :]
            carry = carry + flux[x + 1, padded, :]
            m = []
            for i in range(Q):
                at = ROW + h + VELOCITY[i][1]
                m.append(shift_z(mid[i, x + 1 + VELOCITY[i][0], at : at + 8, :], VELOCITY[i][2]))
            value, gradient = back_tiles(
                m, flow[0, x, rows, :], [flow[1 + a, x, rows, :] for a in range(3)], kind,
                factor_of(kind, fine[x + 2, padded, :]),
            )
            for i in range(Q):
                adjoint[i, x, rows, :] = value[i]
            both = (first[x + 1, padded, :] + gradient) * raw_scale
            raw[x, rows, :] = jnp.where(kind == 1.0, both, 0.0)
        send(x).start()
        return carry

    totals = (*totals, lax.fori_loop(0, BX, last_plane, empty))
    row = jnp.zeros((8, NZ), F32)
    for r, value in enumerate(totals):
        row = jnp.where(lanes((8, NZ)) == r, jnp.sum(value, axis=(0, 1), keepdims=True), row)
    part[...] = row
    for out, begin in ((up_out, BX - RAD), (down_out, 0)):
        for j in range(RAD):
            out[j * BY : (j + 1) * BY, :] = raw[begin + j]
        out[RAW_ROWS:, :] = row
    for x in range(BX):
        send(x).wait()


def main(fwd, later, design, node, region, xlow, xhigh, far, near):
    ins = (fwd, later, design, node, region, xlow, xhigh, far, near)
    specs = [whole(x.shape) for x in ins]
    specs[1] = anywhere()
    outs = [(Q, BX, BY, NZ), (BX, BY, NZ), (8, NZ), (RAW_ROWS + 8, NZ), (RAW_ROWS + 8, NZ)]
    return call(
        main_body,
        outs,
        ins,
        specs,
        scratch=(
            pltpu.VMEM((MSG, BX, NZ), F32),
            pltpu.VMEM((MSG, BX, NZ), F32),
            pltpu.VMEM((BX + 2 * DEEP, PADY, NZ), F32),
            pltpu.VMEM((RAD + 1, BX + 2 * DEEP, 24, NZ), F32),
            pltpu.VMEM((EX, PADY, NZ), F32),
            pltpu.VMEM((EX, PADY, NZ), F32),
            pltpu.VMEM((Q, EX, PADY, NZ), F32),
            pltpu.VMEM((Q, EX, PADY, NZ), F32),
            pltpu.VMEM((Q, BX + 2, PADY, NZ), F32),
            pltpu.VMEM((4, BX, BY, NZ), F32),
            pltpu.VMEM((BX + 2, PADY, NZ), F32),
            pltpu.VMEM((BX + 2, PADY, NZ), F32),
            pltpu.VMEM((Q, BX, BY, NZ), F32),
            pltpu.SemaphoreType.DMA,
            pltpu.SemaphoreType.DMA((BX,)),
        ),
        flops=30000000,
        name="main",
        out_specs=[anywhere()] + [whole(o) for o in outs[1:]],
    )


def raw_y_body(raw, part, low, high, far_out, near_out, rows_out, up_out, down_out):
    for out, begin in ((up_out, BY - RAD), (down_out, 0)):
        out[...] = jnp.zeros_like(out)
        for j in range(RAD):
            y = begin + j
            out[j, RAD : RAD + BX, :] = raw[:, y, :]
            for x in range(RAD):
                out[j, x : x + 1, :] = low[x * BY + y : x * BY + y + 1, :]
                out[j, RAD + BX + x : RAD + BX + x + 1, :] = high[x * BY + y : x * BY + y + 1, :]
    by_parity("gy", up_out, down_out, far_out, near_out)
    other = jnp.where(odd("gx") == 1, low[RAW_ROWS : RAW_ROWS + 8, :], high[RAW_ROWS : RAW_ROWS + 8, :])
    row = part[...] + other
    for k in range(0, rows_out.shape[0], 8):
        rows_out[k : k + 8, :] = row


def raw_y(raw, part, low, high, count):
    ins = (raw, part, low, high)
    return call(
        raw_y_body,
        [(RAD, BY, NZ), (RAD, BY, NZ), (count, NZ)],
        ins,
        [whole(x.shape) for x in ins],
        scratch=(pltpu.VMEM((RAD, BY, NZ), F32),) * 2,
        flops=20000,
        name="raw_y",
    )


def spread_body(raw, xlow, xhigh, far, near, out, ylow, yhigh, wide, folded):
    to_sides("gy", far, near, ylow, yhigh)
    wide[RAD : RAD + BX, ROW : ROW + BY, :] = raw[...]
    for j in range(RAD):
        wide[j, ROW : ROW + BY, :] = xlow[j * BY : (j + 1) * BY, :]
        wide[RAD + BX + j, ROW : ROW + BY, :] = xhigh[j * BY : (j + 1) * BY, :]
    for x in range(BX + 2 * RAD):
        for j in range(RAD):
            wide[x, ROW - RAD + j : ROW - RAD + j + 1, :] = ylow[j, x : x + 1, :]
            wide[x, ROW + BY + j : ROW + BY + j + 1, :] = yhigh[j, x : x + 1, :]

    fold_rows(wide, folded, (ROW, ROW + 8))

    def plane(x, carry):
        for h in (0, 8):
            out[x, h : h + 8, :] = filter_rows(lambda a, b: folded[b, x + RAD + a, h : h + 8, :])
        return carry

    lax.fori_loop(0, BX, plane, 0)


def finish_body(rows, objective, volumes):
    total = add_all(rows[k : k + 8, :] for k in range(0, rows.shape[0], 8))
    lane = lanes((8, NZ))
    for r in range(REG + 1):
        value = jnp.sum(jnp.where(lane == r, total, 0.0))
        if r < REG:
            volumes[r] = value
        else:
            objective[0] = value


def finish(rows):
    return call(
        finish_body,
        [(1,), (REG,)],
        (rows,),
        [whole(rows.shape)],
        flops=100000,
        name="finish",
        out_specs=[scalar(), scalar()],
    )


def spread(raw, xlow, xhigh, far, near):
    ins = (raw, xlow, xhigh, far, near)
    return call(
        spread_body,
        [(BX, BY, NZ)],
        ins,
        [whole(x.shape) for x in ins],
        scratch=(pltpu.VMEM((RAD, BY, NZ), F32),) * 2
        + (pltpu.VMEM((BX + 2 * RAD, PADY, NZ), F32), pltpu.VMEM((RAD + 1, BX + 2 * RAD, BY, NZ), F32)),
        flops=2000000,
        name="spread",
    )[0]


def exchange(up, down, axis):
    count = lax.axis_size(axis)
    forward = [(i, (i + 1) % count) for i in range(count)]
    backward = [(j, i) for i, j in forward]
    return lax.ppermute(up, axis, forward), lax.ppermute(down, axis, backward)


def swap(far, near, axis):
    count = lax.axis_size(axis)
    inner = [(i, i ^ 1) for i in range(count)]
    outer = [(i, (i + 1 if i % 2 else i - 1) % count) for i in range(count)]
    return lax.ppermute(far, axis, outer), lax.ppermute(near, axis, inner)


def share(rows):
    nx, ny = lax.axis_size("gx"), lax.axis_size("gy")
    groups = [[x * ny + y for x in range(p, nx, 2) for y in range(ny)] for p in (0, 1)]
    return lax.all_to_all(rows, ("gx", "gy"), 0, 0, tiled=True, axis_index_groups=groups)


def per_device(forward_pops, later_adjoint, design, node_type, region):
    far, near = swap(*first_y(forward_pops, later_adjoint, design, node_type), "gy")
    own_up, own_down = first_x(forward_pops, later_adjoint, design, node_type)
    xlow, xhigh = exchange(*join_x(own_up, own_down, far, near), "gx")
    adjoint, raw, part, up, down = main(
        forward_pops, later_adjoint, design, node_type, region, xlow, xhigh, far, near
    )
    xlow, xhigh = exchange(up, down, "gx")
    pairs = lax.axis_size("gx") * lax.axis_size("gy") // 2
    far, near, rows = raw_y(raw, part, xlow, xhigh, pairs)
    rows = share(rows)
    far, near = swap(far, near, "gy")
    sensitivity = spread(raw, xlow, xhigh, far, near)
    objective, volumes = finish(rows)
    return adjoint, sensitivity, objective[0], volumes


def solution(mesh):
    cells = P("gx", "gy", None)
    pops = P(None, "gx", "gy", None)
    return jax.shard_map(
        per_device,
        mesh=mesh,
        in_specs=(pops, pops, cells, cells, cells),
        out_specs=(pops, cells, P(), P()),
        check_vma=False,
    )
```
